32 devices in a mesh: dp: 4 (over z), expert: 8 (over y, x, core).
Axes of the slice: x: 2, y: 2, z: 4, core: 2. Of those that a mesh axis runs over, the one named last changes fastest.
Arguments:
- tokens: bfloat16 [4096, 1536], P(('dp', 'expert')), may hold values from -6 to 6
- routes: int32 [4096, 2], P(('dp', 'expert')), may hold values from 0 to 7, all different within a row; in each aligned block of 128 rows (0 to 127, 128 to 255, ...) at most 40 rows name the same one
- combine: float32 [4096, 2], P(('dp', 'expert')), may hold values from 0.1 to 1
- w_gate: bfloat16 [8, 1536, 1536], P('expert', None, 'dp'), may hold values from -0.15625 to 0.15625
- w_up: bfloat16 [8, 1536, 1536], P('expert', None, 'dp'), may hold values from -0.15625 to 0.15625
- w_down: bfloat16 [8, 1536, 1536], P('expert', 'dp'), may hold values from -0.15625 to 0.15625
- cotangent: bfloat16 [4096, 1536], P(('dp', 'expert')), may hold values from -2 to 2
Outputs:
- out: bfloat16 [4096, 1536], P(('dp', 'expert'))
- d_tokens: bfloat16 [4096, 1536], P(('dp', 'expert'))
- d_combine: float32 [4096, 2], P(('dp', 'expert'))
- grad_gate: bfloat16 [8, 1536, 1536], P('expert', None, 'dp')
- grad_up: bfloat16 [8, 1536, 1536], P('expert', None, 'dp')
- grad_down: bfloat16 [8, 1536, 1536], P('expert', 'dp')
The draws below stay inside these ranges and needn't reach their ends.
Inputs may be any that keep to these rules, and one draw needn't show every extreme that they name: `routes`: the two experts of a token differ. Among the 128 tokens of one source block no expert is named more than 40 times, and in every draw some expert is named exactly 40 times by some source block.
All inputs are finite; a program needn't handle non-finite values.
Results may differ from the reference program's by a relative error of at most 0.013.
Values may be sent and summed in bfloat16 or wider, within the bound.
A program may use at most 128 MiB of HBM per device.

```python
import math
import jax
import jax.numpy as jnp
import numpy as np
from jax import lax

D = 1536
FF = 1536
TOK_DEV = 128
EXPERTS = 8
CAP = 40
TOKENS = 4096
N_DP = 4
N_EXPERT = 8


def shard_levels(rng, extent, split, low, largest):
    gain, own = 1.0, jax.random.fold_in(rng, 6)
    for dim, blocks in split:
        steps = jnp.exp(jax.random.uniform(jax.random.fold_in(own, dim), (blocks,), jnp.float32, low / len(split), largest / len(split)))
        gain = gain * jnp.repeat(steps, extent[dim] // blocks).reshape([-1 if axis == dim else 1 for axis in range(len(extent))])
    return gain


def assign_block(key, own, number, rows, count, top, reach, lean):
    sequence = jax.random.permutation(key, count)
    heavy_load, usual = portions_of(count, rows * top, reach, lean, True), portions_of(count, rows * top, reach, lean, False)
    places = jnp.arange(count)

    def named(sizes, turn):
        used = int((sizes > 0).sum())
        fixed = max(1, used // 4)
        moved = fixed + (places - fixed + turn * (used - fixed)) % max(1, count - fixed)
        return jnp.zeros((count,), jnp.int32).at[sequence[jnp.where(places < fixed, places, moved)]].set(jnp.asarray(sizes, jnp.int32))

    sizes = jnp.where(number % 4 == 0, named(heavy_load, number // 4), named(usual, number - number // 4 - 1))
    mixed = jax.random.permutation(jax.random.fold_in(own, 3), count)
    giver, receiver = mixed[0:count // 2 * 2:2], mixed[1:count // 2 * 2:2]
    margin = jnp.minimum(sizes[giver] - 1, reach - sizes[receiver]) // 2
    margin = jnp.where((giver == sequence[0]) | (receiver == sequence[0]) | (sizes[receiver] == 0), 0, jnp.maximum(margin, 0))
    moved = jax.random.randint(jax.random.fold_in(own, 4), (count // 2,), 0, 1 << 20) % (margin + 1)
    sizes = sizes.at[giver].add(-moved).at[receiver].add(moved)
    labels = jnp.searchsorted(jnp.cumsum(sizes), jnp.arange(rows * top), side="right").astype(jnp.int32)
    table = labels.reshape(top, rows).T
    table = table[jax.random.permutation(jax.random.fold_in(own, 1), rows)]
    turn = jax.random.randint(jax.random.fold_in(own, 2), (rows, 1), 0, top)
    return jnp.take_along_axis(table, (jnp.arange(top)[None, :] + turn) % top, axis=1)


def portions_of(number_of, total, most, skew, full):
    weights = [(1 << 20) // math.isqrt(rank ** skew) + 1 for rank in range(1, number_of + 1)]
    largest = most if full else min(most, max(-(-total // number_of), total * weights[0] // sum(weights)))
    least = 1 if total - largest >= number_of - 1 else 0
    counts, rest = [largest] + [least] * (number_of - 1), total - largest - least * (number_of - 1)
    while rest > 0:
        candidates = [i for i in range(1, number_of) if counts[i] < largest] or [i for i in range(1, number_of) if counts[i] < most]
        mass, remaining = sum([weights[i] for i in candidates]), rest
        for i in candidates:
            addition = min(most - counts[i], max(1, remaining * weights[i] // mass), rest)
            counts[i] = counts[i] + addition
            rest = rest - addition
    return np.array(counts)


def gaussian(rng, shape, spread, most, pieces=(), held_as=jnp.bfloat16):
    values = spread * jax.random.normal(rng, shape, jnp.float32)
    if pieces:
        values = values * shard_levels(rng, shape, pieces, -0.22, 0.18)
    return jnp.clip(values, -most, most).astype(held_as)


def setup_inputs(seed: int = 0) -> dict:
    key_of = jax.random.split(jax.random.key(seed), 8)
    tokens = gaussian(key_of[0], (TOKENS, D), 1.0, 6.0, ((0, 32),))
    routes_keys = jax.random.split(jax.random.fold_in(key_of[1], 1), TOKENS // TOK_DEV)
    routes_turns = jax.random.permutation(jax.random.fold_in(key_of[1], 3), TOKENS // TOK_DEV)
    routes = jax.vmap(lambda own, number: assign_block(jax.random.fold_in(key_of[1], 2), own, number, TOK_DEV, EXPERTS, 2, CAP, 1))(routes_keys, routes_turns).reshape((TOKENS, 2))
    combine = jnp.clip(0.1 + 0.9 * jax.random.uniform(key_of[2], (TOKENS, 2), jnp.float32) ** shard_levels(key_of[2], (TOKENS, 2), ((0, 32),), -0.2, 0.2), 0.1, 1.0)
    w_gate = gaussian(key_of[3], (EXPERTS, D, FF), D ** -0.5, 0.15625, ((0, 8), (2, 4)))
    w_up = gaussian(key_of[4], (EXPERTS, D, FF), D ** -0.5, 0.15625, ((0, 8), (2, 4)))
    w_down = gaussian(key_of[5], (EXPERTS, FF, D), FF ** -0.5, 0.15625, ((0, 8), (1, 4)))
    cotangent = gaussian(key_of[6], (TOKENS, D), 0.3, 2.0, ((0, 32),))
    return {"tokens": tokens, "routes": routes, "combine": combine, "w_gate": w_gate, "w_up": w_up, "w_down": w_down, "cotangent": cotangent}


def block_slots(block_routes):
    ids = jnp.arange(EXPERTS, dtype=jnp.int32)
    onehot = (block_routes[:, None] == ids[None, :]).astype(jnp.int32)
    before = jnp.cumsum(onehot, axis=0) - onehot
    return jnp.sum(before * onehot, axis=1).astype(jnp.int32)


def group_total(left, right):
    left_groups = left.astype(jnp.float32).reshape(N_DP, -1, left.shape[1])
    right_groups = right.astype(jnp.float32).reshape(N_DP, -1, right.shape[1])
    part = jnp.einsum("gri,grj->gij", left_groups, right_groups)
    part = lax.optimization_barrier(part.astype(jnp.bfloat16)).astype(jnp.float32)
    return jnp.sum(part, axis=0).astype(jnp.bfloat16)


def reference(tokens, routes, combine, w_gate, w_up, w_down, cotangent):
    pair_count = 2 * TOKENS
    slots = lax.map(block_slots, routes.reshape(N_DP * N_EXPERT, 2 * TOK_DEV)).reshape(-1)
    flat = routes.reshape(-1).astype(jnp.int32)
    pairs = jnp.arange(pair_count, dtype=jnp.int32)
    target_row = (pairs // (2 * TOK_DEV)) * CAP + slots
    table = jnp.full((EXPERTS, N_DP * N_EXPERT * CAP), pair_count, jnp.int32)
    table = table.at[flat, target_row].set(pairs)
    combine_flat = combine.reshape(-1)

    def expert_step(carry, inputs):
        out_acc, back_acc, comb_acc = carry
        table_row, gate_w, up_w, down_w = inputs
        valid = table_row < pair_count
        safe = jnp.minimum(table_row, pair_count - 1).astype(jnp.int32)
        token_index = (safe // 2).astype(jnp.int32)
        weight = jnp.where(valid, combine_flat[safe], jnp.zeros((), combine_flat.dtype))
        token_rows = jnp.where(valid[:, None], tokens[token_index], jnp.zeros((), tokens.dtype))
        cot = cotangent[token_index].astype(jnp.float32)
        gate_pre = jnp.dot(token_rows, gate_w, preferred_element_type=jnp.float32)
        up_pre = jnp.dot(token_rows, up_w, preferred_element_type=jnp.float32)
        sigmoid_gate = jax.nn.sigmoid(gate_pre)
        hidden = (gate_pre * sigmoid_gate * up_pre).astype(jnp.bfloat16)
        expert_out = jnp.dot(hidden, down_w, preferred_element_type=jnp.float32).astype(jnp.bfloat16)
        result = expert_out.astype(jnp.float32)
        landing = jnp.where(valid, token_index, TOKENS).astype(jnp.int32)
        out_acc = out_acc.at[landing].add(weight[:, None] * result, mode="drop")
        dot_terms = jnp.sum(cot * result, axis=1)
        comb_acc = comb_acc.at[jnp.where(valid, table_row, pair_count).astype(jnp.int32)].set(dot_terms, mode="drop")
        cot_rows = (weight[:, None] * cot).astype(jnp.bfloat16)
        d_hidden = jnp.dot(cot_rows, down_w.T, preferred_element_type=jnp.float32)
        d_gate = (d_hidden * up_pre * sigmoid_gate * (1.0 + gate_pre * (1.0 - sigmoid_gate))).astype(jnp.bfloat16)
        d_up = (d_hidden * gate_pre * sigmoid_gate).astype(jnp.bfloat16)
        back_rows = (jnp.dot(d_gate, gate_w.T, preferred_element_type=jnp.float32)
                     + jnp.dot(d_up, up_w.T, preferred_element_type=jnp.float32)).astype(jnp.bfloat16)
        back_acc = back_acc.at[landing].add(back_rows.astype(jnp.float32), mode="drop")
        grads = (group_total(token_rows, d_gate), group_total(token_rows, d_up), group_total(hidden, cot_rows))
        return (out_acc, back_acc, comb_acc), grads

    start = (jnp.zeros((TOKENS, D), jnp.float32), jnp.zeros((TOKENS, D), jnp.float32),
             jnp.zeros((pair_count,), jnp.float32))
    final, grads = lax.scan(expert_step, start, (table, w_gate, w_up, w_down))
    out_acc, back_acc, comb_acc = final
    grad_gate, grad_up, grad_down = grads
    return (out_acc.astype(jnp.bfloat16), back_acc.astype(jnp.bfloat16), comb_acc.reshape(TOKENS, 2),
            grad_gate, grad_up, grad_down)
```

```python
import functools

import jax
import jax.numpy as jnp
from jax import lax
from jax.experimental import pallas as pl
from jax.experimental.pallas import tpu as pltpu
from jax.sharding import PartitionSpec as P

MESH = pl.DeviceIdType.MESH


def greet(groups, experts, d, e):
    barrier = pltpu.get_barrier_semaphore()
    for k in range(1, experts):
        pl.semaphore_signal(
            barrier, inc=1, device_id={"expert": lax.rem(e + k, experts)}, device_id_type=MESH
        )

    @pl.when(d > 0)
    def _():
        pl.semaphore_signal(barrier, inc=1, device_id={"dp": d - 1}, device_id_type=MESH)

    @pl.when(d < groups - 1)
    def _():
        pl.semaphore_signal(barrier, inc=1, device_id={"dp": d + 1}, device_id_type=MESH)

    beside = (d > 0).astype(jnp.int32) + (d < groups - 1).astype(jnp.int32)
    pl.semaphore_wait(barrier, experts - 1 + beside)


def picks(meta, expert, capacity):
    count = meta.shape[1]
    rows = lax.broadcasted_iota(jnp.int32, (capacity, count), 0) + expert * capacity
    rows = rows.astype(jnp.float32)
    return rows == meta[0:1, :], rows == meta[1:2, :]


def dispatch_kernel(
    groups, experts, capacity, tok_ref, cot_ref, meta_ref, tok_all, cot_all, cot_group, meta_all,
    landed, meta_in, staged, line_send, line_recv, plane_send, plane_recv, local_sem, keep_sem,
):
    d = lax.axis_index("dp")
    e = lax.axis_index("expert")
    greet(groups, experts, d, e)
    own = (tok_ref, cot_ref, meta_ref)
    full = (tok_all, cot_all)

    def line_copy(a, s, way, hop, first):
        there = meta_in.at[s] if a == 2 else landed.at[a, s]
        return pltpu.make_async_remote_copy(
            src_ref=own[a] if first else there,
            dst_ref=there,
            send_sem=line_send.at[a, way, hop],
            recv_sem=line_recv.at[a, way, hop],
            device_id={"dp": d + 1 - 2 * way},
            device_id_type=MESH,
        )

    def plane_copy(a, s, k):
        other = lax.rem(e + k, experts)
        return pltpu.make_async_remote_copy(
            src_ref=staged.at[a, s, other],
            dst_ref=full[a].at[s, e],
            send_sem=plane_send.at[a, s, k],
            recv_sem=plane_recv.at[a, s, k],
            device_id={"expert": other},
            device_id_type=MESH,
        )

    def local_copy(a, s):
        return pltpu.make_async_copy(staged.at[a, s, e], full[a].at[s, e], local_sem.at[a, s])

    def keep_copy(s):
        return pltpu.make_async_copy(landed.at[1, s], cot_group.at[s], keep_sem.at[s])

    def process(a, s, source, meta_view):
        def rows_of(other):
            meta = meta_view[...]
            first, second = picks(meta, other, capacity)
            onehot = (first | second).astype(jnp.bfloat16)
            rows = jnp.dot(onehot, source[...], preferred_element_type=jnp.float32)
            if a == 1:
                weight = jnp.sum(
                    jnp.where(first, meta[2:3, :], 0.0) + jnp.where(second, meta[3:4, :], 0.0),
                    axis=1,
                    keepdims=True,
                )
                rows = rows * weight
            staged[a, s, other] = rows.astype(jnp.bfloat16)

        def step(k, carry):
            rows_of(lax.rem(e + k, experts))
            plane_copy(a, s, k).start()
            return carry

        lax.fori_loop(1, experts, step, 0)
        rows_of(e)
        local_copy(a, s).start()

    has_way = (d < groups - 1, d > 0)
    for a in (2, 0, 1):
        for way in (0, 1):

            @pl.when(has_way[way])
            def _(a=a, way=way):
                line_copy(a, d, way, 1, True).start()

    landed[1, d] = cot_ref[...]
    meta_in[d] = meta_ref[...]
    keep_copy(d).start()
    process(0, d, tok_ref, meta_ref)
    process(1, d, cot_ref, meta_ref)
    for hop in range(1, groups):
        for way in (0, 1):
            s = d - hop + 2 * hop * way
            came = (d - hop >= 0) if way == 0 else (d + hop < groups)

            @pl.when(came)
            def _(s=s, way=way, hop=hop):
                for a in (2, 0, 1):
                    line_copy(a, s, way, hop, False).wait_recv()
                    if hop < groups - 1:

                        @pl.when(has_way[way])
                        def _():
                            line_copy(a, s, way, hop + 1, False).start()

                    if a < 2:
                        process(a, s, landed.at[a, s], meta_in.at[s])
                keep_copy(s).start()

    for way in (0, 1):

        @pl.when(has_way[way])
        def _(way=way):
            for a in range(3):
                line_copy(a, d, way, 1, True).wait_send()

        for hop in range(1, groups - 1):
            s = d - hop + 2 * hop * way
            came = (d - hop >= 0) if way == 0 else (d + hop < groups)

            @pl.when(came & has_way[way])
            def _(way=way, hop=hop, s=s):
                for a in range(3):
                    line_copy(a, s, way, hop + 1, False).wait_send()

    def drain(s, carry):
        keep_copy(s).wait()
        for a in (0, 1):
            local_copy(a, s).wait()

            def one(k, inner, a=a):
                plane_copy(a, s, k).wait()
                return inner

            lax.fori_loop(1, experts, one, 0)
        return carry

    lax.fori_loop(0, groups, drain, 0)
    meta_all[...] = meta_in[...]


def dispatch(groups, experts, capacity, tokens, cotangent, meta):
    count, width = tokens.shape
    table = jax.ShapeDtypeStruct((groups, experts, capacity, width), tokens.dtype)
    anywhere = pl.BlockSpec(memory_space=pl.ANY)
    vmem = pl.BlockSpec(memory_space=pltpu.VMEM)
    dma = pltpu.SemaphoreType.DMA
    return pl.pallas_call(
        functools.partial(dispatch_kernel, groups, experts, capacity),
        out_shape=(
            table,
            table,
            jax.ShapeDtypeStruct((groups, count, width), tokens.dtype),
            jax.ShapeDtypeStruct((groups,) + meta.shape, meta.dtype),
        ),
        in_specs=[vmem, vmem, vmem],
        out_specs=(anywhere, anywhere, anywhere, vmem),
        scratch_shapes=[
            pltpu.VMEM((2, groups, count, width), tokens.dtype),
            pltpu.VMEM((groups,) + meta.shape, meta.dtype),
            pltpu.VMEM((2, groups, experts, capacity, width), tokens.dtype),
            dma((3, 2, groups)),
            dma((3, 2, groups)),
            dma((2, groups, experts)),
            dma((2, groups, experts)),
            dma((2, groups)),
            dma((groups,)),
        ],
        compiler_params=pltpu.CompilerParams(
            collective_id=0, has_side_effects=True, vmem_limit_bytes=56 << 20
        ),
        name="dispatch",
    )(tokens, cotangent, meta)


def return_kernel(
    groups, experts, capacity, out_rows, back_rows, cot_group, meta_ref, out_ref, back_ref, dc_ref,
    landed, sums, dc_sums, line_in, dc_in, plane_send, plane_recv, local_sem,
    line_send, line_recv,
):
    d = lax.axis_index("dp")
    e = lax.axis_index("expert")
    greet(groups, experts, d, e)
    parts = (out_rows, back_rows)
    count = cot_group.shape[1]
    width = cot_group.shape[2]

    def target(t):
        low = d < groups - d - 1
        m = jnp.where(low, d, groups - 1 - d)
        j = jnp.where(t < groups - 1 - m, groups - 1 - t, t - (groups - 1 - m))
        j = jnp.where(t == groups - 1, m, j)
        return jnp.where(low, j, groups - 1 - j)

    def plane_copy(a, t, k):
        other = lax.rem(e + k, experts)
        return pltpu.make_async_remote_copy(
            src_ref=parts[a].at[target(t), other],
            dst_ref=landed.at[a, t, e],
            send_sem=plane_send.at[a, t, k],
            recv_sem=plane_recv.at[a, t, k],
            device_id={"expert": other},
            device_id_type=MESH,
        )

    def local_copy(a, t):
        return pltpu.make_async_copy(
            parts[a].at[target(t), e], landed.at[a, t, e], local_sem.at[a, t]
        )

    def line_copy(a, j, way):
        return pltpu.make_async_remote_copy(
            src_ref=dc_sums.at[j] if a == 2 else sums.at[a, j],
            dst_ref=dc_in.at[way, j] if a == 2 else line_in.at[a, way, j],
            send_sem=line_send.at[a, way, j],
            recv_sem=line_recv.at[a, way, j],
            device_id={"dp": d + 1 - 2 * way},
            device_id_type=MESH,
        )

    for t in range(groups):
        for a in (0, 1):

            def begin(k, carry, a=a, t=t):
                plane_copy(a, t, k).start()
                return carry

            lax.fori_loop(1, experts, begin, 0)
            local_copy(a, t).start()

    def gathered(a, t, meta, which):
        total = None
        for other in range(experts):
            first, second = picks(meta, other, capacity)
            mask = (first, second, first | second)[which].astype(jnp.bfloat16)
            term = lax.dot_general(
                mask,
                landed[a, t, other],
                (((0,), (0,)), ((), ())),
                preferred_element_type=jnp.float32,
            )
            total = term if total is None else total + term
        return total

    for t in range(groups):
        j = target(t)
        meta = meta_ref[j]
        for a in (0, 1):
            local_copy(a, t).wait()

            def arrive(k, carry, a=a, t=t):
                plane_copy(a, t, k).wait()
                return carry

            lax.fori_loop(1, experts, arrive, 0)
            if a == 0:
                lane = lax.broadcasted_iota(jnp.int32, (count, 128), 1)
                cot = cot_group[j].astype(jnp.float32)
                weights = jnp.transpose(meta)
                mixed = None
                dots = jnp.zeros((count, 128), jnp.float32)
                for which in (0, 1):
                    rows = gathered(0, t, meta, which)
                    dot = jnp.sum(cot * rows, axis=1, keepdims=True)
                    dots = jnp.where(lane == which, dot, dots)
                    term = weights[:, 2 + which : 3 + which] * rows
                    mixed = term if mixed is None else mixed + term
                dc_sums[j] = dots
                sums[0, j] = mixed.astype(jnp.bfloat16)
            else:
                sums[1, j] = gathered(1, t, meta, 2).astype(jnp.bfloat16)
            for b in (0, 2) if a == 0 else (1,):

                def add(way, b=b, j=j):
                    line_copy(b, j, way).wait_recv()
                    if b == 2:
                        dc_sums[j] = dc_sums[j] + dc_in[way, j]
                    else:
                        sums[b, j] = (
                            sums[b, j].astype(jnp.float32) + line_in[b, way, j].astype(jnp.float32)
                        ).astype(jnp.bfloat16)

                @pl.when((j >= d) & (d > 0))
                def _(add=add):
                    add(0)

                @pl.when((j <= d) & (d < groups - 1))
                def _(add=add):
                    add(1)

                @pl.when(j > d)
                def _(b=b, j=j):
                    line_copy(b, j, 0).start()

                @pl.when(j < d)
                def _(b=b, j=j):
                    line_copy(b, j, 1).start()

    out_ref[...] = sums[0, d]
    back_ref[...] = sums[1, d]
    dc_ref[...] = dc_sums[d]
    for j in range(groups):
        for b in range(3):

            @pl.when(j > d)
            def _(b=b, j=j):
                line_copy(b, j, 0).wait_send()

            @pl.when(j < d)
            def _(b=b, j=j):
                line_copy(b, j, 1).wait_send()


def give_back(groups, experts, capacity, out_rows, back_rows, cot_group, meta_all):
    count, width = cot_group.shape[1:]
    anywhere = pl.BlockSpec(memory_space=pl.ANY)
    vmem = pl.BlockSpec(memory_space=pltpu.VMEM)
    dma = pltpu.SemaphoreType.DMA
    kind = cot_group.dtype
    return pl.pallas_call(
        functools.partial(return_kernel, groups, experts, capacity),
        out_shape=(
            jax.ShapeDtypeStruct((count, width), kind),
            jax.ShapeDtypeStruct((count, width), kind),
            jax.ShapeDtypeStruct((count, 128), jnp.float32),
        ),
        in_specs=[anywhere, anywhere, vmem, vmem],
        out_specs=(vmem, vmem, vmem),
        scratch_shapes=[
            pltpu.VMEM((2, groups, experts, capacity, width), kind),
            pltpu.VMEM((2, groups, count, width), kind),
            pltpu.VMEM((groups, count, 128), jnp.float32),
            pltpu.VMEM((2, 2, groups, count, width), kind),
            pltpu.VMEM((2, groups, count, 128), jnp.float32),
            dma((2, groups, experts)),
            dma((2, groups, experts)),
            dma((2, groups)),
            dma((3, 2, groups)),
            dma((3, 2, groups)),
        ],
        compiler_params=pltpu.CompilerParams(
            collective_id=1, has_side_effects=True, vmem_limit_bytes=56 << 20
        ),
        name="give_back",
    )(out_rows, back_rows, cot_group, meta_all)


def dot_plain(left, right):
    return jnp.dot(left, right, preferred_element_type=jnp.float32)


def dot_last(left, right):
    return lax.dot_general(
        left, right, (((1,), (1,)), ((), ())), preferred_element_type=jnp.float32
    )


def dot_first(left, right):
    return lax.dot_general(
        left, right, (((0,), (0,)), ((), ())), preferred_element_type=jnp.float32
    )


def group_total(left, right, groups):
    left_groups = left.reshape(groups, -1, left.shape[1])
    right_groups = right.reshape(groups, -1, right.shape[1])
    part = jnp.einsum("gri,grj->gij", left_groups, right_groups, preferred_element_type=jnp.float32)
    part = lax.optimization_barrier(part.astype(jnp.bfloat16)).astype(jnp.float32)
    return jnp.sum(part, axis=0).astype(jnp.bfloat16)


def gate_grads(d_hidden, gate_pre, up_pre, sigmoid_gate):
    d_gate = (d_hidden * up_pre * sigmoid_gate * (1.0 + gate_pre * (1.0 - sigmoid_gate))).astype(
        jnp.bfloat16
    )
    d_up = (d_hidden * gate_pre * sigmoid_gate).astype(jnp.bfloat16)
    return (d_gate, d_up)


def plain_device(tokens, routes, combine, w_gate, w_up, w_down, cotangent):
    experts = lax.axis_size("expert")
    groups = lax.axis_size("dp")
    count = tokens.shape[0]
    width = tokens.shape[1]
    capacity = 10 * count // (4 * experts)
    slot_total = experts * capacity
    flat = routes.reshape(-1)
    onehot = (flat[:, None] == jnp.arange(experts, dtype=jnp.int32)[None, :]).astype(jnp.int32)
    before = jnp.cumsum(onehot, axis=0) - onehot
    target_row = (flat * capacity + jnp.sum(before * onehot, axis=1)).reshape(count, 2)
    positions = jnp.arange(slot_total, dtype=jnp.int32)[:, None]
    pick_first = (positions == target_row[None, :, 0]).astype(jnp.bfloat16)
    pick_second = (positions == target_row[None, :, 1]).astype(jnp.bfloat16)
    pick_both = pick_first + pick_second
    send_rows = dot_plain(pick_both, tokens).astype(jnp.bfloat16).reshape(experts, capacity, width)
    token_rows = lax.all_to_all(
        send_rows, "expert", split_axis=0, concat_axis=0, tiled=True
    ).reshape(slot_total, width)
    local_gate = w_gate[0]
    local_up = w_up[0]
    local_down = w_down[0]
    group_rows = lax.all_gather(token_rows, "dp", axis=0, tiled=True)
    gate_pre = dot_plain(group_rows, local_gate)
    up_pre = dot_plain(group_rows, local_up)
    sigmoid_gate = jax.nn.sigmoid(gate_pre)
    hidden = (gate_pre * sigmoid_gate * up_pre).astype(jnp.bfloat16)
    expert_out = lax.psum_scatter(
        dot_plain(hidden, local_down).astype(jnp.bfloat16), "dp", scatter_dimension=0, tiled=True
    )
    returned = lax.all_to_all(
        expert_out.reshape(experts, capacity, width),
        "expert",
        split_axis=0,
        concat_axis=0,
        tiled=True,
    ).reshape(slot_total, width)
    first_out = dot_first(pick_first, returned)
    second_out = dot_first(pick_second, returned)
    out = (combine[:, 0:1] * first_out + combine[:, 1:2] * second_out).astype(jnp.bfloat16)
    cot = cotangent.astype(jnp.float32)
    d_combine = jnp.stack(
        [jnp.sum(cot * first_out, axis=1), jnp.sum(cot * second_out, axis=1)], axis=1
    )
    first_cot = (combine[:, 0:1] * cot).astype(jnp.bfloat16)
    second_cot = (combine[:, 1:2] * cot).astype(jnp.bfloat16)
    send_cot = (dot_plain(pick_first, first_cot) + dot_plain(pick_second, second_cot)).astype(
        jnp.bfloat16
    )
    cot_rows = lax.all_to_all(
        send_cot.reshape(experts, capacity, width),
        "expert",
        split_axis=0,
        concat_axis=0,
        tiled=True,
    ).reshape(slot_total, width)
    group_cot = lax.all_gather(cot_rows, "dp", axis=0, tiled=True)
    d_hidden = dot_last(group_cot, local_down)
    d_gate, d_up = gate_grads(d_hidden, gate_pre, up_pre, sigmoid_gate)
    back_terms = dot_last(d_gate, local_gate) + dot_last(d_up, local_up)
    back_rows = lax.psum_scatter(
        back_terms.astype(jnp.bfloat16), "dp", scatter_dimension=0, tiled=True
    )
    grad_gate = group_total(group_rows, d_gate, groups)
    grad_up = group_total(group_rows, d_up, groups)
    grad_down = group_total(hidden, group_cot, groups)
    arrived = lax.all_to_all(
        back_rows.reshape(experts, capacity, width),
        "expert",
        split_axis=0,
        concat_axis=0,
        tiled=True,
    ).reshape(slot_total, width)
    d_tokens = dot_first(pick_both, arrived).astype(jnp.bfloat16)
    return (out, d_tokens, d_combine, grad_gate[None], grad_up[None], grad_down[None])


def on_device(tokens, routes, combine, w_gate, w_up, w_down, cotangent):
    experts = lax.axis_size("expert")
    groups = lax.axis_size("dp")
    count, width = tokens.shape
    capacity = 10 * count // (4 * experts)
    if capacity % 8 or count % 128 or width % 128 or groups < 2:
        return plain_device(tokens, routes, combine, w_gate, w_up, w_down, cotangent)
    flat = routes.reshape(-1)
    onehot = (flat[:, None] == jnp.arange(experts, dtype=jnp.int32)[None, :]).astype(jnp.int32)
    before = jnp.cumsum(onehot, axis=0) - onehot
    target_row = (flat * capacity + jnp.sum(before * onehot, axis=1)).reshape(count, 2)
    meta = jnp.concatenate(
        [target_row.astype(jnp.float32).T, combine.T, jnp.zeros((4, count), jnp.float32)], axis=0
    )
    table = (groups, experts, capacity, width)
    tok_all, cot_all, cot_group, meta_all = dispatch(
        groups, experts, capacity, tokens, cotangent, meta
    )
    group_rows = tok_all.reshape(-1, width)
    group_cot = cot_all.reshape(-1, width)
    local_gate = w_gate[0]
    local_up = w_up[0]
    local_down = w_down[0]
    gate_pre = dot_plain(group_rows, local_gate)
    up_pre = dot_plain(group_rows, local_up)
    sigmoid_gate = jax.nn.sigmoid(gate_pre)
    hidden = (gate_pre * sigmoid_gate * up_pre).astype(jnp.bfloat16)
    out_part = dot_plain(hidden, local_down).astype(jnp.bfloat16)
    d_hidden = dot_last(group_cot, local_down)
    d_gate, d_up = gate_grads(d_hidden, gate_pre, up_pre, sigmoid_gate)
    back_part = (dot_last(d_gate, local_gate) + dot_last(d_up, local_up)).astype(jnp.bfloat16)
    out, d_tokens, dots = give_back(
        groups, experts, capacity, out_part.reshape(table), back_part.reshape(table),
        cot_group, meta_all,
    )
    grad_gate = dot_first(group_rows, d_gate).astype(jnp.bfloat16)
    grad_up = dot_first(group_rows, d_up).astype(jnp.bfloat16)
    grad_down = dot_first(hidden, group_cot).astype(jnp.bfloat16)
    return (out, d_tokens, dots[:, :2], grad_gate[None], grad_up[None], grad_down[None])


def solution(mesh):
    placed = (
        P(("dp", "expert"), None),
        P(("dp", "expert"), None),
        P(("dp", "expert"), None),
        P("expert", None, "dp"),
        P("expert", None, "dp"),
        P("expert", "dp", None),
        P(("dp", "expert"), None),
    )
    return jax.shard_map(
        on_device,
        mesh=mesh,
        in_specs=placed,
        out_specs=(
            P(("dp", "expert"), None),
            P(("dp", "expert"), None),
            P(("dp", "expert"), None),
            P("expert", None, "dp"),
            P("expert", None, "dp"),
            P("expert", "dp", None),
        ),
        check_vma=False,
    )
```

```python
import functools

import jax
import jax.numpy as jnp
from jax import lax
from jax.experimental import pallas as pl
from jax.experimental.pallas import tpu as pltpu
from jax.sharding import PartitionSpec as P

MESH = pl.DeviceIdType.MESH


def greet(groups, experts, d, e):
    barrier = pltpu.get_barrier_semaphore()
    for k in range(1, experts):
        pl.semaphore_signal(
            barrier, inc=1, device_id={"expert": lax.rem(e + k, experts)}, device_id_type=MESH
        )

    @pl.when(d > 0)
    def _():
        pl.semaphore_signal(barrier, inc=1, device_id={"dp": d - 1}, device_id_type=MESH)

    @pl.when(d < groups - 1)
    def _():
        pl.semaphore_signal(barrier, inc=1, device_id={"dp": d + 1}, device_id_type=MESH)

    beside = (d > 0).astype(jnp.int32) + (d < groups - 1).astype(jnp.int32)
    pl.semaphore_wait(barrier, experts - 1 + beside)


def split(width):
    half = width // 256 * 128
    return (slice(0, half), slice(half, width))


def picks(meta, expert, capacity):
    count = meta.shape[1]
    rows = lax.broadcasted_iota(jnp.int32, (capacity, count), 0) + expert * capacity
    rows = rows.astype(jnp.float32)
    return rows == meta[0:1, :], rows == meta[1:2, :]


def dispatch_kernel(
    groups, experts, capacity, tok_ref, cot_ref, meta_ref, tok_all, cot_all, cot_group, meta_all,
    landed, meta_in, staged, line_send, line_recv, plane_send, plane_recv, local_sem, keep_sem,
    table_send, table_recv,
):
    d = lax.axis_index("dp")
    e = lax.axis_index("expert")
    greet(groups, experts, d, e)
    own = (tok_ref, cot_ref, meta_ref)
    partner = d + 1 - 2 * lax.rem(d, 2)
    halves = split(tok_ref.shape[1])
    full = (tok_all, cot_all)

    def line_copy(a, s, way, hop, first):
        there = meta_in.at[s] if a == 2 else landed.at[a, s]
        return pltpu.make_async_remote_copy(
            src_ref=own[a] if first else there,
            dst_ref=there,
            send_sem=line_send.at[a, way, hop],
            recv_sem=line_recv.at[a, way, hop],
            device_id={"dp": d + 1 - 2 * way},
            device_id_type=MESH,
        )

    def plane_copy(h, a, s, k):
        other = lax.rem(e + k, experts)
        return pltpu.make_async_remote_copy(
            src_ref=staged.at[a, s, other, :, halves[h]],
            dst_ref=full[a].at[s, e, :, halves[h]],
            send_sem=plane_send.at[h, a, s, k],
            recv_sem=plane_recv.at[h, a, s, k],
            device_id={"expert": other},
            device_id_type=MESH,
        )

    def local_copy(h, a, s):
        return pltpu.make_async_copy(
            staged.at[a, s, e, :, halves[h]], full[a].at[s, e, :, halves[h]], local_sem.at[h, a, s]
        )

    def table_copy(a, k):
        source = lax.rem(e + experts - k, experts)
        block = full[a].at[d, source, :, halves[0]]
        return pltpu.make_async_remote_copy(
            src_ref=staged.at[a, d, e, :, halves[0]] if isinstance(k, int) else block,
            dst_ref=block,
            send_sem=table_send.at[a, k],
            recv_sem=table_recv.at[a, k],
            device_id={"dp": partner},
            device_id_type=MESH,
        )

    def hand_over(a):
        def one(k, carry):
            plane_copy(0, a, d, k).wait_recv()
            table_copy(a, k).start()
            return carry

        table_copy(a, 0).start()
        lax.fori_loop(1, experts, one, 0)

    def keep_copy(s):
        return pltpu.make_async_copy(landed.at[1, s], cot_group.at[s], keep_sem.at[s])

    def process(a, s, source, meta_view):
        def rows_of(other):
            meta = meta_view[...]
            first, second = picks(meta, other, capacity)
            onehot = (first | second).astype(jnp.bfloat16)
            rows = jnp.dot(onehot, source[...], preferred_element_type=jnp.float32)
            if a == 1:
                weight = jnp.sum(
                    jnp.where(first, meta[2:3, :], 0.0) + jnp.where(second, meta[3:4, :], 0.0),
                    axis=1,
                    keepdims=True,
                )
                rows = rows * weight
            staged[a, s, other] = rows.astype(jnp.bfloat16)

        def step(k, carry):
            rows_of(lax.rem(e + k, experts))
            plane_copy(1, a, s, k).start()

            @pl.when(s != partner)
            def _():
                plane_copy(0, a, s, k).start()

            return carry

        lax.fori_loop(1, experts, step, 0)
        rows_of(e)
        local_copy(1, a, s).start()

        @pl.when(s != partner)
        def _():
            local_copy(0, a, s).start()

    has_way = (d < groups - 1, d > 0)
    for a in (2, 0, 1):
        for way in (0, 1):

            @pl.when(has_way[way])
            def _(a=a, way=way):
                line_copy(a, d, way, 1, True).start()

    landed[1, d] = cot_ref[...]
    meta_in[d] = meta_ref[...]
    keep_copy(d).start()
    process(0, d, tok_ref, meta_ref)
    process(1, d, cot_ref, meta_ref)
    for hop in range(1, groups):
        for way in (0, 1):
            s = d - hop + 2 * hop * way
            came = (d - hop >= 0) if way == 0 else (d + hop < groups)

            @pl.when(came)
            def _(s=s, way=way, hop=hop):
                for a in (2, 0, 1):
                    line_copy(a, s, way, hop, False).wait_recv()
                    if hop < groups - 1:

                        @pl.when(has_way[way])
                        def _():
                            line_copy(a, s, way, hop + 1, False).start()

                    if a < 2:
                        process(a, s, landed.at[a, s], meta_in.at[s])
                keep_copy(s).start()

        if hop < 3:
            hand_over(hop - 1)

    for a in range(min(groups - 1, 2), 2):
        hand_over(a)

    for way in (0, 1):

        @pl.when(has_way[way])
        def _(way=way):
            for a in range(3):
                line_copy(a, d, way, 1, True).wait_send()

        for hop in range(1, groups - 1):
            s = d - hop + 2 * hop * way
            came = (d - hop >= 0) if way == 0 else (d + hop < groups)

            @pl.when(came & has_way[way])
            def _(way=way, hop=hop, s=s):
                for a in range(3):
                    line_copy(a, s, way, hop + 1, False).wait_send()

    def drain(s, carry):
        keep_copy(s).wait()
        for a in (0, 1):
            local_copy(1, a, s).wait()

            @pl.when(s != partner)
            def _(a=a):
                local_copy(0, a, s).wait()

            def one(k, inner, a=a):
                plane_copy(1, a, s, k).wait()

                @pl.when(s != partner)
                def _():
                    plane_copy(0, a, s, k).wait_send()

                @pl.when((s != partner) & (s != d))
                def _():
                    plane_copy(0, a, s, k).wait_recv()

                return inner

            lax.fori_loop(1, experts, one, 0)
        return carry

    lax.fori_loop(0, groups, drain, 0)

    def tables(k, carry):
        for a in (0, 1):
            table_copy(a, k).wait()
        return carry

    lax.fori_loop(0, experts, tables, 0)
    meta_all[...] = meta_in[...]


def dispatch(groups, experts, capacity, tokens, cotangent, meta):
    count, width = tokens.shape
    table = jax.ShapeDtypeStruct((groups, experts, capacity, width), tokens.dtype)
    anywhere = pl.BlockSpec(memory_space=pl.ANY)
    vmem = pl.BlockSpec(memory_space=pltpu.VMEM)
    dma = pltpu.SemaphoreType.DMA
    return pl.pallas_call(
        functools.partial(dispatch_kernel, groups, experts, capacity),
        out_shape=(
            table,
            table,
            jax.ShapeDtypeStruct((groups, count, width), tokens.dtype),
            jax.ShapeDtypeStruct((groups,) + meta.shape, meta.dtype),
        ),
        in_specs=[vmem, vmem, vmem],
        out_specs=(anywhere, anywhere, anywhere, vmem),
        scratch_shapes=[
            pltpu.VMEM((2, groups, count, width), tokens.dtype),
            pltpu.VMEM((groups,) + meta.shape, meta.dtype),
            pltpu.VMEM((2, groups, experts, capacity, width), tokens.dtype),
            dma((3, 2, groups)),
            dma((3, 2, groups)),
            dma((2, 2, groups, experts)),
            dma((2, 2, groups, experts)),
            dma((2, 2, groups)),
            dma((groups,)),
            dma((2, experts)),
            dma((2, experts)),
        ],
        compiler_params=pltpu.CompilerParams(
            collective_id=0, has_side_effects=True, vmem_limit_bytes=56 << 20
        ),
        name="dispatch",
    )(tokens, cotangent, meta)


def return_kernel(
    groups, experts, capacity, out_rows, back_rows, cot_group, meta_ref, out_ref, back_ref, dc_ref,
    landed, sums, dc_sums, line_in, dc_in, plane_send, plane_recv, local_sem,
    line_send, line_recv, table_in, table_own, table_send, table_recv, table_sem,
):
    d = lax.axis_index("dp")
    e = lax.axis_index("expert")
    greet(groups, experts, d, e)
    parts = (out_rows, back_rows)
    count = cot_group.shape[1]
    halves = split(cot_group.shape[2])
    partner = d + 1 - 2 * lax.rem(d, 2)

    def target(t):
        low = d < groups - d - 1
        m = jnp.where(low, d, groups - 1 - d)
        j = jnp.where(t < groups - 1 - m, groups - 1 - t, t - (groups - 1 - m))
        j = jnp.where(t == groups - 1, m, j)
        return jnp.where(low, j, groups - 1 - j)

    def rows_for(h, a, t, other):
        if h == 0 and t == groups - 1:
            return table_own.at[a, other]
        return parts[a].at[target(t), other, :, halves[h]]

    def plane_copy(h, a, t, k):
        other = lax.rem(e + k, experts)
        return pltpu.make_async_remote_copy(
            src_ref=rows_for(h, a, t, other),
            dst_ref=landed.at[a, t, e, :, halves[h]],
            send_sem=plane_send.at[h, a, t, k],
            recv_sem=plane_recv.at[h, a, t, k],
            device_id={"expert": other},
            device_id_type=MESH,
        )

    def local_copy(h, a, t):
        return pltpu.make_async_copy(
            rows_for(h, a, t, e), landed.at[a, t, e, :, halves[h]], local_sem.at[h, a, t]
        )

    def send_rows(h, a, t):
        def begin(k, carry):
            plane_copy(h, a, t, k).start()
            return carry

        lax.fori_loop(1, experts, begin, 0)
        local_copy(h, a, t).start()

    def await_rows(h, a, t):
        def arrive(k, carry):
            plane_copy(h, a, t, k).wait()
            return carry

        local_copy(h, a, t).wait()
        lax.fori_loop(1, experts, arrive, 0)

    def table_copy(a):
        return pltpu.make_async_remote_copy(
            src_ref=parts[a].at[partner, :, :, halves[0]],
            dst_ref=table_in.at[a],
            send_sem=table_send.at[a],
            recv_sem=table_recv.at[a],
            device_id={"dp": partner},
            device_id_type=MESH,
        )

    def own_table(a):
        return pltpu.make_async_copy(
            parts[a].at[d, :, :, halves[0]], table_own.at[a], table_sem.at[a]
        )

    def line_copy(a, j, way):
        return pltpu.make_async_remote_copy(
            src_ref=dc_sums.at[j] if a == 2 else sums.at[a, j],
            dst_ref=dc_in.at[way, j] if a == 2 else line_in.at[a, way, j],
            send_sem=line_send.at[a, way, j],
            recv_sem=line_recv.at[a, way, j],
            device_id={"dp": d + 1 - 2 * way},
            device_id_type=MESH,
        )

    for a in (0, 1):
        table_copy(a).start()
        own_table(a).start()
    for t in range(groups):
        for a in (0, 1):
            if t < groups - 1:

                @pl.when(target(t) != partner)
                def _(a=a, t=t):
                    send_rows(0, a, t)

            send_rows(1, a, t)
    for a in (0, 1):
        own_table(a).wait()
        table_copy(a).wait()

        def join(k, carry, a=a):
            mine, other = table_own[a, k], table_in[a, k]
            table_own[a, k] = (mine.astype(jnp.float32) + other.astype(jnp.float32)).astype(
                mine.dtype
            )
            return carry

        lax.fori_loop(0, experts, join, 0)
        send_rows(0, a, groups - 1)

    def gathered(h, a, t, meta, which):
        total = None
        for other in range(experts):
            first, second = picks(meta, other, capacity)
            mask = (first, second, first | second)[which].astype(jnp.bfloat16)
            term = lax.dot_general(
                mask,
                landed[a, t, other, :, halves[h]],
                (((0,), (0,)), ((), ())),
                preferred_element_type=jnp.float32,
            )
            total = term if total is None else total + term
        return total

    def gather_half(h, a, t, j):
        meta = meta_ref[j]
        if a == 1:
            sums[1, j, :, halves[h]] = gathered(h, 1, t, meta, 2).astype(jnp.bfloat16)
            return
        lane = lax.broadcasted_iota(jnp.int32, (count, 128), 1)
        cot = cot_group[j, :, halves[h]].astype(jnp.float32)
        weights = jnp.transpose(meta)
        mixed = None
        dots = jnp.zeros((count, 128), jnp.float32)
        for which in (0, 1):
            rows = gathered(h, 0, t, meta, which)
            dot = jnp.sum(cot * rows, axis=1, keepdims=True)
            dots = jnp.where(lane == which, dot, dots)
            term = weights[:, 2 + which : 3 + which] * rows
            mixed = term if mixed is None else mixed + term
        dc_sums[j] = dc_sums[j] + dots
        sums[0, j, :, halves[h]] = mixed.astype(jnp.bfloat16)

    dc_sums[...] = jnp.zeros_like(dc_sums)
    for t in range(groups):
        j = target(t)
        for a in (0, 1):

            @pl.when(j == partner)
            def _(a=a, j=j):
                sums[a, j, :, halves[0]] = jnp.zeros((count, halves[0].stop), sums.dtype)

            @pl.when(j != partner)
            def _(a=a, t=t, j=j):
                await_rows(0, a, t)
                gather_half(0, a, t, j)

            await_rows(1, a, t)
            gather_half(1, a, t, j)
            for b in (0, 2) if a == 0 else (1,):

                def add(way, b=b, j=j):
                    line_copy(b, j, way).wait_recv()
                    if b == 2:
                        dc_sums[j] = dc_sums[j] + dc_in[way, j]
                    else:
                        sums[b, j] = (
                            sums[b, j].astype(jnp.float32) + line_in[b, way, j].astype(jnp.float32)
                        ).astype(jnp.bfloat16)

                @pl.when((j >= d) & (d > 0))
                def _(add=add):
                    add(0)

                @pl.when((j <= d) & (d < groups - 1))
                def _(add=add):
                    add(1)

                @pl.when(j > d)
                def _(b=b, j=j):
                    line_copy(b, j, 0).start()

                @pl.when(j < d)
                def _(b=b, j=j):
                    line_copy(b, j, 1).start()

    out_ref[...] = sums[0, d]
    back_ref[...] = sums[1, d]
    dc_ref[...] = dc_sums[d]
    for j in range(groups):
        for b in range(3):

            @pl.when(j > d)
            def _(b=b, j=j):
                line_copy(b, j, 0).wait_send()

            @pl.when(j < d)
            def _(b=b, j=j):
                line_copy(b, j, 1).wait_send()


def give_back(groups, experts, capacity, out_rows, back_rows, cot_group, meta_all):
    count, width = cot_group.shape[1:]
    anywhere = pl.BlockSpec(memory_space=pl.ANY)
    vmem = pl.BlockSpec(memory_space=pltpu.VMEM)
    dma = pltpu.SemaphoreType.DMA
    kind = cot_group.dtype
    return pl.pallas_call(
        functools.partial(return_kernel, groups, experts, capacity),
        out_shape=(
            jax.ShapeDtypeStruct((count, width), kind),
            jax.ShapeDtypeStruct((count, width), kind),
            jax.ShapeDtypeStruct((count, 128), jnp.float32),
        ),
        in_specs=[anywhere, anywhere, vmem, vmem],
        out_specs=(vmem, vmem, vmem),
        scratch_shapes=[
            pltpu.VMEM((2, groups, experts, capacity, width), kind),
            pltpu.VMEM((2, groups, count, width), kind),
            pltpu.VMEM((groups, count, 128), jnp.float32),
            pltpu.VMEM((2, 2, groups, count, width), kind),
            pltpu.VMEM((2, groups, count, 128), jnp.float32),
            dma((2, 2, groups, experts)),
            dma((2, 2, groups, experts)),
            dma((2, 2, groups)),
            dma((3, 2, groups)),
            dma((3, 2, groups)),
            pltpu.VMEM((2, experts, capacity, split(width)[0].stop), kind),
            pltpu.VMEM((2, experts, capacity, split(width)[0].stop), kind),
            dma((2,)),
            dma((2,)),
            dma((2,)),
        ],
        compiler_params=pltpu.CompilerParams(
            collective_id=1, has_side_effects=True, vmem_limit_bytes=56 << 20
        ),
        name="give_back",
    )(out_rows, back_rows, cot_group, meta_all)


def dot_plain(left, right):
    return jnp.dot(left, right, preferred_element_type=jnp.float32)


def dot_last(left, right):
    return lax.dot_general(
        left, right, (((1,), (1,)), ((), ())), preferred_element_type=jnp.float32
    )


def dot_first(left, right):
    return lax.dot_general(
        left, right, (((0,), (0,)), ((), ())), preferred_element_type=jnp.float32
    )


def group_total(left, right, groups):
    left_groups = left.reshape(groups, -1, left.shape[1])
    right_groups = right.reshape(groups, -1, right.shape[1])
    part = jnp.einsum("gri,grj->gij", left_groups, right_groups, preferred_element_type=jnp.float32)
    part = lax.optimization_barrier(part.astype(jnp.bfloat16)).astype(jnp.float32)
    return jnp.sum(part, axis=0).astype(jnp.bfloat16)


def gate_grads(d_hidden, gate_pre, up_pre, sigmoid_gate):
    d_gate = (d_hidden * up_pre * sigmoid_gate * (1.0 + gate_pre * (1.0 - sigmoid_gate))).astype(
        jnp.bfloat16
    )
    d_up = (d_hidden * gate_pre * sigmoid_gate).astype(jnp.bfloat16)
    return (d_gate, d_up)


def plain_device(tokens, routes, combine, w_gate, w_up, w_down, cotangent):
    experts = lax.axis_size("expert")
    groups = lax.axis_size("dp")
    count = tokens.shape[0]
    width = tokens.shape[1]
    capacity = 10 * count // (4 * experts)
    slot_total = experts * capacity
    flat = routes.reshape(-1)
    onehot = (flat[:, None] == jnp.arange(experts, dtype=jnp.int32)[None, :]).astype(jnp.int32)
    before = jnp.cumsum(onehot, axis=0) - onehot
    target_row = (flat * capacity + jnp.sum(before * onehot, axis=1)).reshape(count, 2)
    positions = jnp.arange(slot_total, dtype=jnp.int32)[:, None]
    pick_first = (positions == target_row[None, :, 0]).astype(jnp.bfloat16)
    pick_second = (positions == target_row[None, :, 1]).astype(jnp.bfloat16)
    pick_both = pick_first + pick_second
    send_rows = dot_plain(pick_both, tokens).astype(jnp.bfloat16).reshape(experts, capacity, width)
    token_rows = lax.all_to_all(
        send_rows, "expert", split_axis=0, concat_axis=0, tiled=True
    ).reshape(slot_total, width)
    local_gate = w_gate[0]
    local_up = w_up[0]
    local_down = w_down[0]
    group_rows = lax.all_gather(token_rows, "dp", axis=0, tiled=True)
    gate_pre = dot_plain(group_rows, local_gate)
    up_pre = dot_plain(group_rows, local_up)
    sigmoid_gate = jax.nn.sigmoid(gate_pre)
    hidden = (gate_pre * sigmoid_gate * up_pre).astype(jnp.bfloat16)
    expert_out = lax.psum_scatter(
        dot_plain(hidden, local_down).astype(jnp.bfloat16), "dp", scatter_dimension=0, tiled=True
    )
    returned = lax.all_to_all(
        expert_out.reshape(experts, capacity, width),
        "expert",
        split_axis=0,
        concat_axis=0,
        tiled=True,
    ).reshape(slot_total, width)
    first_out = dot_first(pick_first, returned)
    second_out = dot_first(pick_second, returned)
    out = (combine[:, 0:1] * first_out + combine[:, 1:2] * second_out).astype(jnp.bfloat16)
    cot = cotangent.astype(jnp.float32)
    d_combine = jnp.stack(
        [jnp.sum(cot * first_out, axis=1), jnp.sum(cot * second_out, axis=1)], axis=1
    )
    first_cot = (combine[:, 0:1] * cot).astype(jnp.bfloat16)
    second_cot = (combine[:, 1:2] * cot).astype(jnp.bfloat16)
    send_cot = (dot_plain(pick_first, first_cot) + dot_plain(pick_second, second_cot)).astype(
        jnp.bfloat16
    )
    cot_rows = lax.all_to_all(
        send_cot.reshape(experts, capacity, width),
        "expert",
        split_axis=0,
        concat_axis=0,
        tiled=True,
    ).reshape(slot_total, width)
    group_cot = lax.all_gather(cot_rows, "dp", axis=0, tiled=True)
    d_hidden = dot_last(group_cot, local_down)
    d_gate, d_up = gate_grads(d_hidden, gate_pre, up_pre, sigmoid_gate)
    back_terms = dot_last(d_gate, local_gate) + dot_last(d_up, local_up)
    back_rows = lax.psum_scatter(
        back_terms.astype(jnp.bfloat16), "dp", scatter_dimension=0, tiled=True
    )
    grad_gate = group_total(group_rows, d_gate, groups)
    grad_up = group_total(group_rows, d_up, groups)
    grad_down = group_total(hidden, group_cot, groups)
    arrived = lax.all_to_all(
        back_rows.reshape(experts, capacity, width),
        "expert",
        split_axis=0,
        concat_axis=0,
        tiled=True,
    ).reshape(slot_total, width)
    d_tokens = dot_first(pick_both, arrived).astype(jnp.bfloat16)
    return (out, d_tokens, d_combine, grad_gate[None], grad_up[None], grad_down[None])


def on_device(tokens, routes, combine, w_gate, w_up, w_down, cotangent):
    experts = lax.axis_size("expert")
    groups = lax.axis_size("dp")
    count, width = tokens.shape
    capacity = 10 * count // (4 * experts)
    if capacity % 8 or count % 128 or width % 128 or width < 256 or groups % 2:
        return plain_device(tokens, routes, combine, w_gate, w_up, w_down, cotangent)
    flat = routes.reshape(-1)
    onehot = (flat[:, None] == jnp.arange(experts, dtype=jnp.int32)[None, :]).astype(jnp.int32)
    before = jnp.cumsum(onehot, axis=0) - onehot
    target_row = (flat * capacity + jnp.sum(before * onehot, axis=1)).reshape(count, 2)
    meta = jnp.concatenate(
        [target_row.astype(jnp.float32).T, combine.T, jnp.zeros((4, count), jnp.float32)], axis=0
    )
    table = (groups, experts, capacity, width)
    tok_all, cot_all, cot_group, meta_all = dispatch(
        groups, experts, capacity, tokens, cotangent, meta
    )
    group_rows = tok_all.reshape(-1, width)
    group_cot = cot_all.reshape(-1, width)
    local_gate = w_gate[0]
    local_up = w_up[0]
    local_down = w_down[0]
    gate_pre = dot_plain(group_rows, local_gate)
    up_pre = dot_plain(group_rows, local_up)
    sigmoid_gate = jax.nn.sigmoid(gate_pre)
    hidden = (gate_pre * sigmoid_gate * up_pre).astype(jnp.bfloat16)
    out_part = dot_plain(hidden, local_down).astype(jnp.bfloat16)
    d_hidden = dot_last(group_cot, local_down)
    d_gate, d_up = gate_grads(d_hidden, gate_pre, up_pre, sigmoid_gate)
    back_part = (dot_last(d_gate, local_gate) + dot_last(d_up, local_up)).astype(jnp.bfloat16)
    out, d_tokens, dots = give_back(
        groups, experts, capacity, out_part.reshape(table), back_part.reshape(table),
        cot_group, meta_all,
    )
    grad_gate = dot_first(group_rows, d_gate).astype(jnp.bfloat16)
    grad_up = dot_first(group_rows, d_up).astype(jnp.bfloat16)
    grad_down = dot_first(hidden, group_cot).astype(jnp.bfloat16)
    return (out, d_tokens, dots[:, :2], grad_gate[None], grad_up[None], grad_down[None])


def solution(mesh):
    placed = (
        P(("dp", "expert"), None),
        P(("dp", "expert"), None),
        P(("dp", "expert"), None),
        P("expert", None, "dp"),
        P("expert", None, "dp"),
        P("expert", "dp", None),
        P(("dp", "expert"), None),
    )
    return jax.shard_map(
        on_device,
        mesh=mesh,
        in_specs=placed,
        out_specs=(
            P(("dp", "expert"), None),
            P(("dp", "expert"), None),
            P(("dp", "expert"), None),
            P("expert", None, "dp"),
            P("expert", None, "dp"),
            P("expert", "dp", None),
        ),
        check_vma=False,
    )
```

```python
import functools

import jax
import jax.numpy as jnp
from jax import lax
from jax.experimental import pallas as pl
from jax.experimental.pallas import tpu as pltpu
from jax.sharding import PartitionSpec as P

MESH = pl.DeviceIdType.MESH


def greet(groups, experts, d, e):
    barrier = pltpu.get_barrier_semaphore()
    for k in range(1, experts):
        pl.semaphore_signal(
            barrier, inc=1, device_id={"expert": lax.rem(e + k, experts)}, device_id_type=MESH
        )

    @pl.when(d > 0)
    def _():
        pl.semaphore_signal(barrier, inc=1, device_id={"dp": d - 1}, device_id_type=MESH)

    @pl.when(d < groups - 1)
    def _():
        pl.semaphore_signal(barrier, inc=1, device_id={"dp": d + 1}, device_id_type=MESH)

    beside = (d > 0).astype(jnp.int32) + (d < groups - 1).astype(jnp.int32)
    pl.semaphore_wait(barrier, experts - 1 + beside)


def split(width):
    half = width // 256 * 128
    return (slice(0, half), slice(half, width))


def picks(meta, expert, capacity):
    count = meta.shape[1]
    rows = lax.broadcasted_iota(jnp.int32, (capacity, count), 0) + expert * capacity
    rows = rows.astype(jnp.float32)
    return rows == meta[0:1, :], rows == meta[1:2, :]


def place(experts, capacity, meta_ref, meta_own):
    count = meta_ref.shape[1]
    meta = meta_ref[...]
    names = lax.broadcasted_iota(jnp.int32, (experts, count), 0).astype(jnp.float32)
    first = (names == meta[0:1, :]).astype(jnp.float32)
    second = (names == meta[1:2, :]).astype(jnp.float32)
    square = (count, count)
    earlier = lax.broadcasted_iota(jnp.int32, square, 0) < lax.broadcasted_iota(jnp.int32, square, 1)
    before = jnp.dot(
        (first + second).astype(jnp.bfloat16),
        earlier.astype(jnp.bfloat16),
        preferred_element_type=jnp.float32,
    )
    meta_own[...] = meta
    for k, chosen in enumerate((first, second)):
        slot = jnp.sum(before * chosen, axis=0, keepdims=True)
        meta_own[k : k + 1, :] = meta[k : k + 1, :] * capacity + slot


def dispatch_kernel(
    groups, experts, capacity, tok_ref, cot_ref, meta_ref, tok_all, cot_all, cot_group, meta_all,
    landed, meta_in, staged, line_send, line_recv, plane_send, plane_recv, local_sem, keep_sem,
    table_send, table_recv, meta_own,
):
    d = lax.axis_index("dp")
    e = lax.axis_index("expert")
    greet(groups, experts, d, e)
    own = (tok_ref, cot_ref, meta_own)
    partner = d + 1 - 2 * lax.rem(d, 2)
    halves = split(tok_ref.shape[1])
    full = (tok_all, cot_all)

    def line_copy(a, s, way, hop, first):
        there = meta_in.at[s] if a == 2 else landed.at[a, s]
        return pltpu.make_async_remote_copy(
            src_ref=own[a] if first else there,
            dst_ref=there,
            send_sem=line_send.at[a, way, hop],
            recv_sem=line_recv.at[a, way, hop],
            device_id={"dp": d + 1 - 2 * way},
            device_id_type=MESH,
        )

    def plane_copy(h, a, s, k):
        other = lax.rem(e + k, experts)
        return pltpu.make_async_remote_copy(
            src_ref=staged.at[a, s, other, :, halves[h]],
            dst_ref=full[a].at[s, e, :, halves[h]],
            send_sem=plane_send.at[h, a, s, k],
            recv_sem=plane_recv.at[h, a, s, k],
            device_id={"expert": other},
            device_id_type=MESH,
        )

    def local_copy(h, a, s):
        return pltpu.make_async_copy(
            staged.at[a, s, e, :, halves[h]], full[a].at[s, e, :, halves[h]], local_sem.at[h, a, s]
        )

    def table_copy(a, k):
        source = lax.rem(e + experts - k, experts)
        block = full[a].at[d, source, :, halves[0]]
        return pltpu.make_async_remote_copy(
            src_ref=staged.at[a, d, e, :, halves[0]] if isinstance(k, int) else block,
            dst_ref=block,
            send_sem=table_send.at[a, k],
            recv_sem=table_recv.at[a, k],
            device_id={"dp": partner},
            device_id_type=MESH,
        )

    def hand_over(a):
        def one(k, carry):
            plane_copy(0, a, d, k).wait_recv()
            table_copy(a, k).start()
            return carry

        table_copy(a, 0).start()
        lax.fori_loop(1, experts, one, 0)

    def keep_copy(s):
        return pltpu.make_async_copy(landed.at[1, s], cot_group.at[s], keep_sem.at[s])

    def process(a, s, source, meta_view):
        meta = meta_view[...]
        first, second = picks(meta, 0, experts * capacity)
        onehot = (first | second).astype(jnp.bfloat16)
        if a == 1:
            weight = jnp.sum(
                jnp.where(first, meta[2:3, :], 0.0) + jnp.where(second, meta[3:4, :], 0.0),
                axis=1,
                keepdims=True,
            )
        for half in halves:
            rows = jnp.dot(onehot, source[:, half], preferred_element_type=jnp.float32)
            if a == 1:
                rows = rows * weight
            for other in range(experts):
                staged[a, s, other, :, half] = rows[
                    other * capacity : (other + 1) * capacity
                ].astype(jnp.bfloat16)

        def step(k, carry):
            plane_copy(1, a, s, k).start()

            @pl.when(s != partner)
            def _():
                plane_copy(0, a, s, k).start()

            return carry

        lax.fori_loop(1, experts, step, 0)
        local_copy(1, a, s).start()

        @pl.when(s != partner)
        def _():
            local_copy(0, a, s).start()

    has_way = (d < groups - 1, d > 0)
    for a in (0, 1, 2):
        if a == 2:
            place(experts, capacity, meta_ref, meta_own)
        for way in (0, 1):

            @pl.when(has_way[way])
            def _(a=a, way=way):
                line_copy(a, d, way, 1, True).start()

    landed[1, d] = cot_ref[...]
    meta_in[d] = meta_own[...]
    keep_copy(d).start()
    process(0, d, tok_ref, meta_own)
    process(1, d, cot_ref, meta_own)
    for hop in range(1, groups):
        for way in (0, 1):
            s = d - hop + 2 * hop * way
            came = (d - hop >= 0) if way == 0 else (d + hop < groups)

            @pl.when(came)
            def _(s=s, way=way, hop=hop):
                for a in (2, 0, 1):
                    line_copy(a, s, way, hop, False).wait_recv()
                    if hop < groups - 1:

                        @pl.when(has_way[way])
                        def _():
                            line_copy(a, s, way, hop + 1, False).start()

                    if a < 2:
                        process(a, s, landed.at[a, s], meta_in.at[s])
                keep_copy(s).start()

        if hop < 3:
            hand_over(hop - 1)

    for a in range(min(groups - 1, 2), 2):
        hand_over(a)

    for way in (0, 1):

        @pl.when(has_way[way])
        def _(way=way):
            for a in range(3):
                line_copy(a, d, way, 1, True).wait_send()

        for hop in range(1, groups - 1):
            s = d - hop + 2 * hop * way
            came = (d - hop >= 0) if way == 0 else (d + hop < groups)

            @pl.when(came & has_way[way])
            def _(way=way, hop=hop, s=s):
                for a in range(3):
                    line_copy(a, s, way, hop + 1, False).wait_send()

    def drain(s, carry):
        keep_copy(s).wait()
        for a in (0, 1):
            local_copy(1, a, s).wait()

            @pl.when(s != partner)
            def _(a=a):
                local_copy(0, a, s).wait()

            def one(k, inner, a=a):
                plane_copy(1, a, s, k).wait()

                @pl.when(s != partner)
                def _():
                    plane_copy(0, a, s, k).wait_send()

                @pl.when((s != partner) & (s != d))
                def _():
                    plane_copy(0, a, s, k).wait_recv()

                return inner

            lax.fori_loop(1, experts, one, 0)
        return carry

    lax.fori_loop(0, groups, drain, 0)

    def tables(k, carry):
        for a in (0, 1):
            table_copy(a, k).wait()
        return carry

    lax.fori_loop(0, experts, tables, 0)
    meta_all[...] = meta_in[...]


def dispatch(groups, experts, capacity, tokens, cotangent, meta):
    count, width = tokens.shape
    table = jax.ShapeDtypeStruct((groups, experts, capacity, width), tokens.dtype)
    anywhere = pl.BlockSpec(memory_space=pl.ANY)
    vmem = pl.BlockSpec(memory_space=pltpu.VMEM)
    dma = pltpu.SemaphoreType.DMA
    return pl.pallas_call(
        functools.partial(dispatch_kernel, groups, experts, capacity),
        out_shape=(
            table,
            table,
            jax.ShapeDtypeStruct((groups, count, width), tokens.dtype),
            jax.ShapeDtypeStruct((groups,) + meta.shape, meta.dtype),
        ),
        in_specs=[vmem, vmem, vmem],
        out_specs=(anywhere, anywhere, anywhere, vmem),
        scratch_shapes=[
            pltpu.VMEM((2, groups, count, width), tokens.dtype),
            pltpu.VMEM((groups,) + meta.shape, meta.dtype),
            pltpu.VMEM((2, groups, experts, capacity, width), tokens.dtype),
            dma((3, 2, groups)),
            dma((3, 2, groups)),
            dma((2, 2, groups, experts)),
            dma((2, 2, groups, experts)),
            dma((2, 2, groups)),
            dma((groups,)),
            dma((2, experts)),
            dma((2, experts)),
            pltpu.VMEM(meta.shape, meta.dtype),
        ],
        compiler_params=pltpu.CompilerParams(
            collective_id=0, has_side_effects=True, vmem_limit_bytes=56 << 20
        ),
        name="dispatch",
    )(tokens, cotangent, meta)


def return_kernel(
    groups, experts, capacity, out_rows, back_rows, cot_group, meta_ref, out_ref, back_ref, dc_ref,
    landed, sums, dc_sums, line_in, dc_in, plane_send, plane_recv, local_sem,
    line_send, line_recv, table_in, table_own, table_send, table_recv, table_sem,
):
    d = lax.axis_index("dp")
    e = lax.axis_index("expert")
    greet(groups, experts, d, e)
    parts = (out_rows, back_rows)
    count = cot_group.shape[1]
    halves = split(cot_group.shape[2])
    partner = d + 1 - 2 * lax.rem(d, 2)

    def target(t):
        low = d < groups - d - 1
        m = jnp.where(low, d, groups - 1 - d)
        j = jnp.where(t < groups - 1 - m, groups - 1 - t, t - (groups - 1 - m))
        j = jnp.where(t == groups - 1, m, j)
        return jnp.where(low, j, groups - 1 - j)

    def rows_for(h, a, t, other):
        if h == 0 and t == groups - 1:
            return table_own.at[a, other]
        return parts[a].at[target(t), other, :, halves[h]]

    def plane_copy(h, a, t, k):
        other = lax.rem(e + k, experts)
        return pltpu.make_async_remote_copy(
            src_ref=rows_for(h, a, t, other),
            dst_ref=landed.at[a, t, e, :, halves[h]],
            send_sem=plane_send.at[h, a, t, k],
            recv_sem=plane_recv.at[h, a, t, k],
            device_id={"expert": other},
            device_id_type=MESH,
        )

    def local_copy(h, a, t):
        return pltpu.make_async_copy(
            rows_for(h, a, t, e), landed.at[a, t, e, :, halves[h]], local_sem.at[h, a, t]
        )

    def send_rows(h, a, t):
        def begin(k, carry):
            plane_copy(h, a, t, k).start()
            return carry

        lax.fori_loop(1, experts, begin, 0)
        local_copy(h, a, t).start()

    def await_rows(h, a, t):
        def arrive(k, carry):
            plane_copy(h, a, t, k).wait()
            return carry

        local_copy(h, a, t).wait()
        lax.fori_loop(1, experts, arrive, 0)

    def table_copy(a):
        return pltpu.make_async_remote_copy(
            src_ref=parts[a].at[partner, :, :, halves[0]],
            dst_ref=table_in.at[a],
            send_sem=table_send.at[a],
            recv_sem=table_recv.at[a],
            device_id={"dp": partner},
            device_id_type=MESH,
        )

    def own_table(a):
        return pltpu.make_async_copy(
            parts[a].at[d, :, :, halves[0]], table_own.at[a], table_sem.at[a]
        )

    def line_copy(a, j, way):
        return pltpu.make_async_remote_copy(
            src_ref=dc_sums.at[j] if a == 2 else sums.at[a, j],
            dst_ref=dc_in.at[way, j] if a == 2 else line_in.at[a, way, j],
            send_sem=line_send.at[a, way, j],
            recv_sem=line_recv.at[a, way, j],
            device_id={"dp": d + 1 - 2 * way},
            device_id_type=MESH,
        )

    for a in (0, 1):
        table_copy(a).start()
        own_table(a).start()
    for t in range(groups):
        for a in (0, 1):
            if t < groups - 1:

                @pl.when(target(t) != partner)
                def _(a=a, t=t):
                    send_rows(0, a, t)

            send_rows(1, a, t)
    for a in (0, 1):
        own_table(a).wait()
        table_copy(a).wait()

        def join(k, carry, a=a):
            mine, other = table_own[a, k], table_in[a, k]
            table_own[a, k] = (mine.astype(jnp.float32) + other.astype(jnp.float32)).astype(
                mine.dtype
            )
            return carry

        lax.fori_loop(0, experts, join, 0)
        send_rows(0, a, groups - 1)

    def gathered(h, a, t, meta, both):
        total = None
        for other in range(experts):
            first, second = picks(meta, other, capacity)
            if both:
                mask = jnp.concatenate(
                    [first.astype(jnp.bfloat16), second.astype(jnp.bfloat16)], axis=1
                )
            else:
                mask = (first | second).astype(jnp.bfloat16)
            term = lax.dot_general(
                mask,
                landed[a, t, other, :, halves[h]],
                (((0,), (0,)), ((), ())),
                preferred_element_type=jnp.float32,
            )
            total = term if total is None else total + term
        return total

    def gather_half(h, a, t, j):
        meta = meta_ref[j]
        if a == 1:
            sums[1, j, :, halves[h]] = gathered(h, 1, t, meta, False).astype(jnp.bfloat16)
            return
        lane = lax.broadcasted_iota(jnp.int32, (count, 128), 1)
        cot = cot_group[j, :, halves[h]].astype(jnp.float32)
        weights = jnp.transpose(meta)
        mixed = None
        dots = jnp.zeros((count, 128), jnp.float32)
        pair = gathered(h, 0, t, meta, True)
        for which in (0, 1):
            rows = pair[which * count : (which + 1) * count]
            dot = jnp.sum(cot * rows, axis=1, keepdims=True)
            dots = jnp.where(lane == which, dot, dots)
            term = weights[:, 2 + which : 3 + which] * rows
            mixed = term if mixed is None else mixed + term
        dc_sums[j] = dc_sums[j] + dots
        sums[0, j, :, halves[h]] = mixed.astype(jnp.bfloat16)

    dc_sums[...] = jnp.zeros_like(dc_sums)
    for t in range(groups):
        j = target(t)
        for a in (0, 1):

            if t == groups - 1:
                if a == 0:
                    for h in (1, 0):
                        for c in (0, 1):
                            await_rows(h, c, t)
                            gather_half(h, c, t, j)
            else:

                @pl.when(j == partner)
                def _(a=a, j=j):
                    sums[a, j, :, halves[0]] = jnp.zeros((count, halves[0].stop), sums.dtype)

                @pl.when(j != partner)
                def _(a=a, t=t, j=j):
                    await_rows(0, a, t)
                    gather_half(0, a, t, j)

                await_rows(1, a, t)
                gather_half(1, a, t, j)
            for b in (0, 2) if a == 0 else (1,):

                def add(way, b=b, j=j):
                    line_copy(b, j, way).wait_recv()
                    if b == 2:
                        dc_sums[j] = dc_sums[j] + dc_in[way, j]
                    else:
                        sums[b, j] = (
                            sums[b, j].astype(jnp.float32) + line_in[b, way, j].astype(jnp.float32)
                        ).astype(jnp.bfloat16)

                @pl.when((j >= d) & (d > 0))
                def _(add=add):
                    add(0)

                @pl.when((j <= d) & (d < groups - 1))
                def _(add=add):
                    add(1)

                @pl.when(j > d)
                def _(b=b, j=j):
                    line_copy(b, j, 0).start()

                @pl.when(j < d)
                def _(b=b, j=j):
                    line_copy(b, j, 1).start()

    out_ref[...] = sums[0, d]
    back_ref[...] = sums[1, d]
    dc_ref[...] = dc_sums[d]
    for j in range(groups):
        for b in range(3):

            @pl.when(j > d)
            def _(b=b, j=j):
                line_copy(b, j, 0).wait_send()

            @pl.when(j < d)
            def _(b=b, j=j):
                line_copy(b, j, 1).wait_send()


def give_back(groups, experts, capacity, out_rows, back_rows, cot_group, meta_all):
    count, width = cot_group.shape[1:]
    anywhere = pl.BlockSpec(memory_space=pl.ANY)
    vmem = pl.BlockSpec(memory_space=pltpu.VMEM)
    dma = pltpu.SemaphoreType.DMA
    kind = cot_group.dtype
    return pl.pallas_call(
        functools.partial(return_kernel, groups, experts, capacity),
        out_shape=(
            jax.ShapeDtypeStruct((count, width), kind),
            jax.ShapeDtypeStruct((count, width), kind),
            jax.ShapeDtypeStruct((count, 128), jnp.float32),
        ),
        in_specs=[anywhere, anywhere, vmem, vmem],
        out_specs=(vmem, vmem, vmem),
        scratch_shapes=[
            pltpu.VMEM((2, groups, experts, capacity, width), kind),
            pltpu.VMEM((2, groups, count, width), kind),
            pltpu.VMEM((groups, count, 128), jnp.float32),
            pltpu.VMEM((2, 2, groups, count, width), kind),
            pltpu.VMEM((2, groups, count, 128), jnp.float32),
            dma((2, 2, groups, experts)),
            dma((2, 2, groups, experts)),
            dma((2, 2, groups)),
            dma((3, 2, groups)),
            dma((3, 2, groups)),
            pltpu.VMEM((2, experts, capacity, split(width)[0].stop), kind),
            pltpu.VMEM((2, experts, capacity, split(width)[0].stop), kind),
            dma((2,)),
            dma((2,)),
            dma((2,)),
        ],
        compiler_params=pltpu.CompilerParams(
            collective_id=1, has_side_effects=True, vmem_limit_bytes=56 << 20
        ),
        name="give_back",
    )(out_rows, back_rows, cot_group, meta_all)


def dot_plain(left, right):
    return jnp.dot(left, right, preferred_element_type=jnp.float32)


def dot_last(left, right):
    return lax.dot_general(
        left, right, (((1,), (1,)), ((), ())), preferred_element_type=jnp.float32
    )


def dot_first(left, right):
    return lax.dot_general(
        left, right, (((0,), (0,)), ((), ())), preferred_element_type=jnp.float32
    )


def group_total(left, right, groups):
    left_groups = left.reshape(groups, -1, left.shape[1])
    right_groups = right.reshape(groups, -1, right.shape[1])
    part = jnp.einsum("gri,grj->gij", left_groups, right_groups, preferred_element_type=jnp.float32)
    part = lax.optimization_barrier(part.astype(jnp.bfloat16)).astype(jnp.float32)
    return jnp.sum(part, axis=0).astype(jnp.bfloat16)


def gate_grads(d_hidden, gate_pre, up_pre, sigmoid_gate):
    d_gate = (d_hidden * up_pre * sigmoid_gate * (1.0 + gate_pre * (1.0 - sigmoid_gate))).astype(
        jnp.bfloat16
    )
    d_up = (d_hidden * gate_pre * sigmoid_gate).astype(jnp.bfloat16)
    return (d_gate, d_up)


def plain_device(tokens, routes, combine, w_gate, w_up, w_down, cotangent):
    experts = lax.axis_size("expert")
    groups = lax.axis_size("dp")
    count = tokens.shape[0]
    width = tokens.shape[1]
    capacity = 10 * count // (4 * experts)
    slot_total = experts * capacity
    flat = routes.reshape(-1)
    onehot = (flat[:, None] == jnp.arange(experts, dtype=jnp.int32)[None, :]).astype(jnp.int32)
    before = jnp.cumsum(onehot, axis=0) - onehot
    target_row = (flat * capacity + jnp.sum(before * onehot, axis=1)).reshape(count, 2)
    positions = jnp.arange(slot_total, dtype=jnp.int32)[:, None]
    pick_first = (positions == target_row[None, :, 0]).astype(jnp.bfloat16)
    pick_second = (positions == target_row[None, :, 1]).astype(jnp.bfloat16)
    pick_both = pick_first + pick_second
    send_rows = dot_plain(pick_both, tokens).astype(jnp.bfloat16).reshape(experts, capacity, width)
    token_rows = lax.all_to_all(
        send_rows, "expert", split_axis=0, concat_axis=0, tiled=True
    ).reshape(slot_total, width)
    local_gate = w_gate[0]
    local_up = w_up[0]
    local_down = w_down[0]
    group_rows = lax.all_gather(token_rows, "dp", axis=0, tiled=True)
    gate_pre = dot_plain(group_rows, local_gate)
    up_pre = dot_plain(group_rows, local_up)
    sigmoid_gate = jax.nn.sigmoid(gate_pre)
    hidden = (gate_pre * sigmoid_gate * up_pre).astype(jnp.bfloat16)
    expert_out = lax.psum_scatter(
        dot_plain(hidden, local_down).astype(jnp.bfloat16), "dp", scatter_dimension=0, tiled=True
    )
    returned = lax.all_to_all(
        expert_out.reshape(experts, capacity, width),
        "expert",
        split_axis=0,
        concat_axis=0,
        tiled=True,
    ).reshape(slot_total, width)
    first_out = dot_first(pick_first, returned)
    second_out = dot_first(pick_second, returned)
    out = (combine[:, 0:1] * first_out + combine[:, 1:2] * second_out).astype(jnp.bfloat16)
    cot = cotangent.astype(jnp.float32)
    d_combine = jnp.stack(
        [jnp.sum(cot * first_out, axis=1), jnp.sum(cot * second_out, axis=1)], axis=1
    )
    first_cot = (combine[:, 0:1] * cot).astype(jnp.bfloat16)
    second_cot = (combine[:, 1:2] * cot).astype(jnp.bfloat16)
    send_cot = (dot_plain(pick_first, first_cot) + dot_plain(pick_second, second_cot)).astype(
        jnp.bfloat16
    )
    cot_rows = lax.all_to_all(
        send_cot.reshape(experts, capacity, width),
        "expert",
        split_axis=0,
        concat_axis=0,
        tiled=True,
    ).reshape(slot_total, width)
    group_cot = lax.all_gather(cot_rows, "dp", axis=0, tiled=True)
    d_hidden = dot_last(group_cot, local_down)
    d_gate, d_up = gate_grads(d_hidden, gate_pre, up_pre, sigmoid_gate)
    back_terms = dot_last(d_gate, local_gate) + dot_last(d_up, local_up)
    back_rows = lax.psum_scatter(
        back_terms.astype(jnp.bfloat16), "dp", scatter_dimension=0, tiled=True
    )
    grad_gate = group_total(group_rows, d_gate, groups)
    grad_up = group_total(group_rows, d_up, groups)
    grad_down = group_total(hidden, group_cot, groups)
    arrived = lax.all_to_all(
        back_rows.reshape(experts, capacity, width),
        "expert",
        split_axis=0,
        concat_axis=0,
        tiled=True,
    ).reshape(slot_total, width)
    d_tokens = dot_first(pick_both, arrived).astype(jnp.bfloat16)
    return (out, d_tokens, d_combine, grad_gate[None], grad_up[None], grad_down[None])


def on_device(tokens, routes, combine, w_gate, w_up, w_down, cotangent):
    experts = lax.axis_size("expert")
    groups = lax.axis_size("dp")
    count, width = tokens.shape
    capacity = 10 * count // (4 * experts)
    if capacity % 8 or count % 128 or width % 128 or width < 256 or groups % 2:
        return plain_device(tokens, routes, combine, w_gate, w_up, w_down, cotangent)
    meta = jnp.concatenate(
        [routes.astype(jnp.float32).T, combine.T, jnp.zeros((4, count), jnp.float32)], axis=0
    )
    table = (groups, experts, capacity, width)
    tok_all, cot_all, cot_group, meta_all = dispatch(
        groups, experts, capacity, tokens, cotangent, meta
    )
    group_rows = tok_all.reshape(-1, width)
    group_cot = cot_all.reshape(-1, width)
    local_gate = w_gate[0]
    local_up = w_up[0]
    local_down = w_down[0]
    gate_pre = dot_plain(group_rows, local_gate)
    up_pre = dot_plain(group_rows, local_up)
    sigmoid_gate = jax.nn.sigmoid(gate_pre)
    hidden = (gate_pre * sigmoid_gate * up_pre).astype(jnp.bfloat16)
    out_part = dot_plain(hidden, local_down).astype(jnp.bfloat16)
    d_hidden = dot_last(group_cot, local_down)
    d_gate, d_up = gate_grads(d_hidden, gate_pre, up_pre, sigmoid_gate)
    back_part = (dot_last(d_gate, local_gate) + dot_last(d_up, local_up)).astype(jnp.bfloat16)
    out, d_tokens, dots = give_back(
        groups, experts, capacity, out_part.reshape(table), back_part.reshape(table),
        cot_group, meta_all,
    )
    grad_gate = dot_first(group_rows, d_gate).astype(jnp.bfloat16)
    grad_up = dot_first(group_rows, d_up).astype(jnp.bfloat16)
    grad_down = dot_first(hidden, group_cot).astype(jnp.bfloat16)
    return (out, d_tokens, dots[:, :2], grad_gate[None], grad_up[None], grad_down[None])


def solution(mesh):
    placed = (
        P(("dp", "expert"), None),
        P(("dp", "expert"), None),
        P(("dp", "expert"), None),
        P("expert", None, "dp"),
        P("expert", None, "dp"),
        P("expert", "dp", None),
        P(("dp", "expert"), None),
    )
    return jax.shard_map(
        on_device,
        mesh=mesh,
        in_specs=placed,
        out_specs=(
            P(("dp", "expert"), None),
            P(("dp", "expert"), None),
            P(("dp", "expert"), None),
            P("expert", None, "dp"),
            P("expert", None, "dp"),
            P("expert", "dp", None),
        ),
        check_vma=False,
    )
```

```python
import functools

import jax
import jax.numpy as jnp
from jax import lax
from jax.experimental import pallas as pl
from jax.experimental.pallas import tpu as pltpu
from jax.sharding import PartitionSpec as P

MESH = pl.DeviceIdType.MESH


def greet(groups, experts, d, e):
    barrier = pltpu.get_barrier_semaphore()
    for k in range(1, experts):
        pl.semaphore_signal(
            barrier, inc=1, device_id={"expert": lax.rem(e + k, experts)}, device_id_type=MESH
        )

    @pl.when(d > 0)
    def _():
        pl.semaphore_signal(barrier, inc=1, device_id={"dp": d - 1}, device_id_type=MESH)

    @pl.when(d < groups - 1)
    def _():
        pl.semaphore_signal(barrier, inc=1, device_id={"dp": d + 1}, device_id_type=MESH)

    beside = (d > 0).astype(jnp.int32) + (d < groups - 1).astype(jnp.int32)
    pl.semaphore_wait(barrier, experts - 1 + beside)


def split(width):
    half = width // 384 * 128
    return (slice(0, half), slice(half, width))


def picks(meta, expert, capacity):
    count = meta.shape[1]
    rows = lax.broadcasted_iota(jnp.int32, (capacity, count), 0) + expert * capacity
    rows = rows.astype(jnp.float32)
    return rows == meta[0:1, :], rows == meta[1:2, :]


def place(experts, capacity, meta_ref, meta_own):
    count = meta_ref.shape[1]
    meta = meta_ref[...]
    names = lax.broadcasted_iota(jnp.int32, (experts, count), 0).astype(jnp.float32)
    first = (names == meta[0:1, :]).astype(jnp.float32)
    second = (names == meta[1:2, :]).astype(jnp.float32)
    square = (count, count)
    earlier = lax.broadcasted_iota(jnp.int32, square, 0) < lax.broadcasted_iota(jnp.int32, square, 1)
    before = jnp.dot(
        (first + second).astype(jnp.bfloat16),
        earlier.astype(jnp.bfloat16),
        preferred_element_type=jnp.float32,
    )
    meta_own[...] = meta
    for k, chosen in enumerate((first, second)):
        slot = jnp.sum(before * chosen, axis=0, keepdims=True)
        meta_own[k : k + 1, :] = meta[k : k + 1, :] * capacity + slot


def dispatch_kernel(
    groups, experts, capacity, tok_ref, cot_ref, meta_ref, tok_all, cot_all, cot_group, meta_all,
    landed, meta_in, staged, line_send, line_recv, plane_send, plane_recv, local_sem, keep_sem,
    table_send, table_recv, meta_own,
):
    d = lax.axis_index("dp")
    e = lax.axis_index("expert")
    greet(groups, experts, d, e)
    own = (tok_ref, cot_ref, meta_own)
    partner = d + 1 - 2 * lax.rem(d, 2)
    halves = split(tok_ref.shape[1])
    full = (tok_all, cot_all)

    def line_copy(a, s, way, hop, first):
        there = meta_in.at[s] if a == 2 else landed.at[a, s]
        return pltpu.make_async_remote_copy(
            src_ref=own[a] if first else there,
            dst_ref=there,
            send_sem=line_send.at[a, way, hop],
            recv_sem=line_recv.at[a, way, hop],
            device_id={"dp": d + 1 - 2 * way},
            device_id_type=MESH,
        )

    def plane_copy(h, a, s, k):
        other = lax.rem(e + k, experts)
        return pltpu.make_async_remote_copy(
            src_ref=staged.at[a, s, other, :, halves[h]],
            dst_ref=full[a].at[s, e, :, halves[h]],
            send_sem=plane_send.at[h, a, s, k],
            recv_sem=plane_recv.at[h, a, s, k],
            device_id={"expert": other},
            device_id_type=MESH,
        )

    def local_copy(h, a, s):
        return pltpu.make_async_copy(
            staged.at[a, s, e, :, halves[h]], full[a].at[s, e, :, halves[h]], local_sem.at[h, a, s]
        )

    def table_copy(a, k):
        source = lax.rem(e + experts - k, experts)
        block = full[a].at[d, source, :, halves[0]]
        return pltpu.make_async_remote_copy(
            src_ref=staged.at[a, d, e, :, halves[0]] if isinstance(k, int) else block,
            dst_ref=block,
            send_sem=table_send.at[a, k],
            recv_sem=table_recv.at[a, k],
            device_id={"dp": partner},
            device_id_type=MESH,
        )

    def hand_over(a):
        def one(k, carry):
            plane_copy(0, a, d, k).wait_recv()
            table_copy(a, k).start()
            return carry

        table_copy(a, 0).start()
        lax.fori_loop(1, experts, one, 0)

    def keep_copy(s):
        return pltpu.make_async_copy(landed.at[1, s], cot_group.at[s], keep_sem.at[s])

    def process(a, s, source, meta_view):
        meta = meta_view[...]
        first, second = picks(meta, 0, experts * capacity)
        onehot = (first | second).astype(jnp.bfloat16)
        if a == 1:
            weight = jnp.sum(
                jnp.where(first, meta[2:3, :], 0.0) + jnp.where(second, meta[3:4, :], 0.0),
                axis=1,
                keepdims=True,
            )
        for half in halves:
            rows = jnp.dot(onehot, source[:, half], preferred_element_type=jnp.float32)
            if a == 1:
                rows = rows * weight
            for other in range(experts):
                staged[a, s, other, :, half] = rows[
                    other * capacity : (other + 1) * capacity
                ].astype(jnp.bfloat16)

        def step(k, carry):
            plane_copy(1, a, s, k).start()

            @pl.when(s != partner)
            def _():
                plane_copy(0, a, s, k).start()

            return carry

        lax.fori_loop(1, experts, step, 0)
        local_copy(1, a, s).start()

        @pl.when(s != partner)
        def _():
            local_copy(0, a, s).start()

    has_way = (d < groups - 1, d > 0)
    for a in (0, 1, 2):
        if a == 2:
            place(experts, capacity, meta_ref, meta_own)
        for way in (0, 1):

            @pl.when(has_way[way])
            def _(a=a, way=way):
                line_copy(a, d, way, 1, True).start()

    landed[1, d] = cot_ref[...]
    meta_in[d] = meta_own[...]
    keep_copy(d).start()
    process(0, d, tok_ref, meta_own)
    process(1, d, cot_ref, meta_own)
    for hop in range(1, groups):
        for way in (0, 1):
            s = d - hop + 2 * hop * way
            came = (d - hop >= 0) if way == 0 else (d + hop < groups)

            @pl.when(came)
            def _(s=s, way=way, hop=hop):
                for a in (2, 0, 1):
                    line_copy(a, s, way, hop, False).wait_recv()
                    if hop < groups - 1:

                        @pl.when(has_way[way])
                        def _():
                            line_copy(a, s, way, hop + 1, False).start()

                    if a < 2:
                        process(a, s, landed.at[a, s], meta_in.at[s])
                keep_copy(s).start()

        if hop < 3:
            hand_over(hop - 1)

    for a in range(min(groups - 1, 2), 2):
        hand_over(a)

    for way in (0, 1):

        @pl.when(has_way[way])
        def _(way=way):
            for a in range(3):
                line_copy(a, d, way, 1, True).wait_send()

        for hop in range(1, groups - 1):
            s = d - hop + 2 * hop * way
            came = (d - hop >= 0) if way == 0 else (d + hop < groups)

            @pl.when(came & has_way[way])
            def _(way=way, hop=hop, s=s):
                for a in range(3):
                    line_copy(a, s, way, hop + 1, False).wait_send()

    def drain(s, carry):
        keep_copy(s).wait()
        for a in (0, 1):
            local_copy(1, a, s).wait()

            @pl.when(s != partner)
            def _(a=a):
                local_copy(0, a, s).wait()

            def one(k, inner, a=a):
                plane_copy(1, a, s, k).wait()

                @pl.when(s != partner)
                def _():
                    plane_copy(0, a, s, k).wait_send()

                @pl.when((s != partner) & (s != d))
                def _():
                    plane_copy(0, a, s, k).wait_recv()

                return inner

            lax.fori_loop(1, experts, one, 0)
        return carry

    lax.fori_loop(0, groups, drain, 0)

    def tables(k, carry):
        for a in (0, 1):
            table_copy(a, k).wait()
        return carry

    lax.fori_loop(0, experts, tables, 0)
    meta_all[...] = meta_in[...]


def dispatch(groups, experts, capacity, tokens, cotangent, meta):
    count, width = tokens.shape
    table = jax.ShapeDtypeStruct((groups, experts, capacity, width), tokens.dtype)
    anywhere = pl.BlockSpec(memory_space=pl.ANY)
    vmem = pl.BlockSpec(memory_space=pltpu.VMEM)
    dma = pltpu.SemaphoreType.DMA
    return pl.pallas_call(
        functools.partial(dispatch_kernel, groups, experts, capacity),
        out_shape=(
            table,
            table,
            jax.ShapeDtypeStruct((groups, count, width), tokens.dtype),
            jax.ShapeDtypeStruct((groups,) + meta.shape, meta.dtype),
        ),
        in_specs=[vmem, vmem, vmem],
        out_specs=(anywhere, anywhere, anywhere, vmem),
        scratch_shapes=[
            pltpu.VMEM((2, groups, count, width), tokens.dtype),
            pltpu.VMEM((groups,) + meta.shape, meta.dtype),
            pltpu.VMEM((2, groups, experts, capacity, width), tokens.dtype),
            dma((3, 2, groups)),
            dma((3, 2, groups)),
            dma((2, 2, groups, experts)),
            dma((2, 2, groups, experts)),
            dma((2, 2, groups)),
            dma((groups,)),
            dma((2, experts)),
            dma((2, experts)),
            pltpu.VMEM(meta.shape, meta.dtype),
        ],
        compiler_params=pltpu.CompilerParams(
            collective_id=0, has_side_effects=True, vmem_limit_bytes=56 << 20
        ),
        name="dispatch",
    )(tokens, cotangent, meta)


def return_kernel(
    groups, experts, capacity, out_rows, back_rows, cot_group, meta_ref, out_ref, back_ref, dc_ref,
    landed, sums, dc_sums, line_in, dc_in, plane_send, plane_recv, local_sem,
    line_send, line_recv, table_in, table_own, table_send, table_recv, table_sem,
):
    d = lax.axis_index("dp")
    e = lax.axis_index("expert")
    greet(groups, experts, d, e)
    parts = (out_rows, back_rows)
    count = cot_group.shape[1]
    halves = split(cot_group.shape[2])
    partner = d + 1 - 2 * lax.rem(d, 2)

    def target(t):
        low = d < groups - d - 1
        m = jnp.where(low, d, groups - 1 - d)
        j = jnp.where(t < groups - 1 - m, groups - 1 - t, t - (groups - 1 - m))
        j = jnp.where(t == groups - 1, m, j)
        return jnp.where(low, j, groups - 1 - j)

    def rows_for(h, a, t, other):
        if h == 0 and t == groups - 1:
            return table_own.at[a, other]
        return parts[a].at[target(t), other, :, halves[h]]

    def plane_copy(h, a, t, k):
        other = lax.rem(e + k, experts)
        return pltpu.make_async_remote_copy(
            src_ref=rows_for(h, a, t, other),
            dst_ref=landed.at[a, t, e, :, halves[h]],
            send_sem=plane_send.at[h, a, t, k],
            recv_sem=plane_recv.at[h, a, t, k],
            device_id={"expert": other},
            device_id_type=MESH,
        )

    def local_copy(h, a, t):
        return pltpu.make_async_copy(
            rows_for(h, a, t, e), landed.at[a, t, e, :, halves[h]], local_sem.at[h, a, t]
        )

    def send_rows(h, a, t):
        def begin(k, carry):
            plane_copy(h, a, t, k).start()
            return carry

        lax.fori_loop(1, experts, begin, 0)
        local_copy(h, a, t).start()

    def await_rows(h, a, t):
        def arrive(k, carry):
            plane_copy(h, a, t, k).wait()
            return carry

        local_copy(h, a, t).wait()
        lax.fori_loop(1, experts, arrive, 0)

    def table_copy(a):
        return pltpu.make_async_remote_copy(
            src_ref=parts[a].at[partner, :, :, halves[0]],
            dst_ref=table_in.at[a],
            send_sem=table_send.at[a],
            recv_sem=table_recv.at[a],
            device_id={"dp": partner},
            device_id_type=MESH,
        )

    def own_table(a):
        return pltpu.make_async_copy(
            parts[a].at[d, :, :, halves[0]], table_own.at[a], table_sem.at[a]
        )

    def line_copy(a, j, way):
        return pltpu.make_async_remote_copy(
            src_ref=dc_sums.at[j] if a == 2 else sums.at[a, j],
            dst_ref=dc_in.at[way, j] if a == 2 else line_in.at[a, way, j],
            send_sem=line_send.at[a, way, j],
            recv_sem=line_recv.at[a, way, j],
            device_id={"dp": d + 1 - 2 * way},
            device_id_type=MESH,
        )

    for a in (0, 1):
        table_copy(a).start()
        own_table(a).start()
    for t in range(groups):
        for a in (0, 1):
            if t < groups - 1:

                @pl.when(target(t) != partner)
                def _(a=a, t=t):
                    send_rows(0, a, t)

            send_rows(1, a, t)
    for a in (0, 1):
        own_table(a).wait()
        table_copy(a).wait()

        def join(k, carry, a=a):
            mine, other = table_own[a, k], table_in[a, k]
            table_own[a, k] = (mine.astype(jnp.float32) + other.astype(jnp.float32)).astype(
                mine.dtype
            )
            return carry

        lax.fori_loop(0, experts, join, 0)
        send_rows(0, a, groups - 1)

    def gathered(h, a, t, meta, both):
        total = None
        for other in range(experts):
            first, second = picks(meta, other, capacity)
            if both:
                mask = jnp.concatenate(
                    [first.astype(jnp.bfloat16), second.astype(jnp.bfloat16)], axis=1
                )
            else:
                mask = (first | second).astype(jnp.bfloat16)
            term = lax.dot_general(
                mask,
                landed[a, t, other, :, halves[h]],
                (((0,), (0,)), ((), ())),
                preferred_element_type=jnp.float32,
            )
            total = term if total is None else total + term
        return total

    def gather_half(h, a, t, j):
        meta = meta_ref[j]
        if a == 1:
            sums[1, j, :, halves[h]] = gathered(h, 1, t, meta, False).astype(jnp.bfloat16)
            return
        lane = lax.broadcasted_iota(jnp.int32, (count, 128), 1)
        cot = cot_group[j, :, halves[h]].astype(jnp.float32)
        weights = jnp.transpose(meta)
        mixed = None
        dots = jnp.zeros((count, 128), jnp.float32)
        pair = gathered(h, 0, t, meta, True)
        for which in (0, 1):
            rows = pair[which * count : (which + 1) * count]
            dot = jnp.sum(cot * rows, axis=1, keepdims=True)
            dots = jnp.where(lane == which, dot, dots)
            term = weights[:, 2 + which : 3 + which] * rows
            mixed = term if mixed is None else mixed + term
        dc_sums[j] = dc_sums[j] + dots
        sums[0, j, :, halves[h]] = mixed.astype(jnp.bfloat16)

    dc_sums[...] = jnp.zeros_like(dc_sums)
    for t in range(groups):
        j = target(t)
        for a in (0, 1):

            if t == groups - 1:
                if a == 0:
                    for h in (1, 0):
                        for c in (0, 1):
                            await_rows(h, c, t)
                            gather_half(h, c, t, j)
            else:

                @pl.when(j == partner)
                def _(a=a, j=j):
                    sums[a, j, :, halves[0]] = jnp.zeros((count, halves[0].stop), sums.dtype)

                @pl.when(j != partner)
                def _(a=a, t=t, j=j):
                    await_rows(0, a, t)
                    gather_half(0, a, t, j)

                await_rows(1, a, t)
                gather_half(1, a, t, j)
            for b in (0, 2) if a == 0 else (1,):

                def add(way, b=b, j=j):
                    line_copy(b, j, way).wait_recv()
                    if b == 2:
                        dc_sums[j] = dc_sums[j] + dc_in[way, j]
                    else:
                        sums[b, j] = (
                            sums[b, j].astype(jnp.float32) + line_in[b, way, j].astype(jnp.float32)
                        ).astype(jnp.bfloat16)

                @pl.when((j >= d) & (d > 0))
                def _(add=add):
                    add(0)

                @pl.when((j <= d) & (d < groups - 1))
                def _(add=add):
                    add(1)

                @pl.when(j > d)
                def _(b=b, j=j):
                    line_copy(b, j, 0).start()

                @pl.when(j < d)
                def _(b=b, j=j):
                    line_copy(b, j, 1).start()

    out_ref[...] = sums[0, d]
    back_ref[...] = sums[1, d]
    dc_ref[...] = dc_sums[d]
    for j in range(groups):
        for b in range(3):

            @pl.when(j > d)
            def _(b=b, j=j):
                line_copy(b, j, 0).wait_send()

            @pl.when(j < d)
            def _(b=b, j=j):
                line_copy(b, j, 1).wait_send()


def finish_kernel(out_in, back_in, dots_in, out_ref, back_ref, dots_ref):
    out_ref[...] = out_in[...]
    back_ref[...] = back_in[...]
    dots_ref[...] = jnp.transpose(dots_in[...])[: dots_ref.shape[0]]


def finish(out, back, dots):
    vmem = pl.BlockSpec(memory_space=pltpu.VMEM)
    out, back, dots = pl.pallas_call(
        finish_kernel,
        out_shape=(
            jax.ShapeDtypeStruct(out.shape, out.dtype),
            jax.ShapeDtypeStruct(back.shape, back.dtype),
            jax.ShapeDtypeStruct((2, out.shape[0]), dots.dtype),
        ),
        in_specs=[vmem] * 3,
        out_specs=(vmem,) * 3,
        name="finish",
    )(out, back, dots)
    return out, back, dots.T


def give_back(groups, experts, capacity, out_rows, back_rows, cot_group, meta_all):
    count, width = cot_group.shape[1:]
    anywhere = pl.BlockSpec(memory_space=pl.ANY)
    vmem = pl.BlockSpec(memory_space=pltpu.VMEM)
    dma = pltpu.SemaphoreType.DMA
    kind = cot_group.dtype
    return pl.pallas_call(
        functools.partial(return_kernel, groups, experts, capacity),
        out_shape=(
            jax.ShapeDtypeStruct((count, width), kind),
            jax.ShapeDtypeStruct((count, width), kind),
            jax.ShapeDtypeStruct((count, 128), jnp.float32),
        ),
        in_specs=[anywhere, anywhere, vmem, vmem],
        out_specs=(vmem, vmem, vmem),
        scratch_shapes=[
            pltpu.VMEM((2, groups, experts, capacity, width), kind),
            pltpu.VMEM((2, groups, count, width), kind),
            pltpu.VMEM((groups, count, 128), jnp.float32),
            pltpu.VMEM((2, 2, groups, count, width), kind),
            pltpu.VMEM((2, groups, count, 128), jnp.float32),
            dma((2, 2, groups, experts)),
            dma((2, 2, groups, experts)),
            dma((2, 2, groups)),
            dma((3, 2, groups)),
            dma((3, 2, groups)),
            pltpu.VMEM((2, experts, capacity, split(width)[0].stop), kind),
            pltpu.VMEM((2, experts, capacity, split(width)[0].stop), kind),
            dma((2,)),
            dma((2,)),
            dma((2,)),
        ],
        compiler_params=pltpu.CompilerParams(
            collective_id=1, has_side_effects=True, vmem_limit_bytes=56 << 20
        ),
        name="give_back",
    )(out_rows, back_rows, cot_group, meta_all)


def dot_plain(left, right):
    return jnp.dot(left, right, preferred_element_type=jnp.float32)


def dot_last(left, right):
    return lax.dot_general(
        left, right, (((1,), (1,)), ((), ())), preferred_element_type=jnp.float32
    )


def dot_first(left, right):
    return lax.dot_general(
        left, right, (((0,), (0,)), ((), ())), preferred_element_type=jnp.float32
    )


def group_total(left, right, groups):
    left_groups = left.reshape(groups, -1, left.shape[1])
    right_groups = right.reshape(groups, -1, right.shape[1])
    part = jnp.einsum("gri,grj->gij", left_groups, right_groups, preferred_element_type=jnp.float32)
    part = lax.optimization_barrier(part.astype(jnp.bfloat16)).astype(jnp.float32)
    return jnp.sum(part, axis=0).astype(jnp.bfloat16)


def gate_grads(d_hidden, gate_pre, up_pre, sigmoid_gate):
    d_gate = (d_hidden * up_pre * sigmoid_gate * (1.0 + gate_pre * (1.0 - sigmoid_gate))).astype(
        jnp.bfloat16
    )
    d_up = (d_hidden * gate_pre * sigmoid_gate).astype(jnp.bfloat16)
    return (d_gate, d_up)


def plain_device(tokens, routes, combine, w_gate, w_up, w_down, cotangent):
    experts = lax.axis_size("expert")
    groups = lax.axis_size("dp")
    count = tokens.shape[0]
    width = tokens.shape[1]
    capacity = 10 * count // (4 * experts)
    slot_total = experts * capacity
    flat = routes.reshape(-1)
    onehot = (flat[:, None] == jnp.arange(experts, dtype=jnp.int32)[None, :]).astype(jnp.int32)
    before = jnp.cumsum(onehot, axis=0) - onehot
    target_row = (flat * capacity + jnp.sum(before * onehot, axis=1)).reshape(count, 2)
    positions = jnp.arange(slot_total, dtype=jnp.int32)[:, None]
    pick_first = (positions == target_row[None, :, 0]).astype(jnp.bfloat16)
    pick_second = (positions == target_row[None, :, 1]).astype(jnp.bfloat16)
    pick_both = pick_first + pick_second
    send_rows = dot_plain(pick_both, tokens).astype(jnp.bfloat16).reshape(experts, capacity, width)
    token_rows = lax.all_to_all(
        send_rows, "expert", split_axis=0, concat_axis=0, tiled=True
    ).reshape(slot_total, width)
    local_gate = w_gate[0]
    local_up = w_up[0]
    local_down = w_down[0]
    group_rows = lax.all_gather(token_rows, "dp", axis=0, tiled=True)
    gate_pre = dot_plain(group_rows, local_gate)
    up_pre = dot_plain(group_rows, local_up)
    sigmoid_gate = jax.nn.sigmoid(gate_pre)
    hidden = (gate_pre * sigmoid_gate * up_pre).astype(jnp.bfloat16)
    expert_out = lax.psum_scatter(
        dot_plain(hidden, local_down).astype(jnp.bfloat16), "dp", scatter_dimension=0, tiled=True
    )
    returned = lax.all_to_all(
        expert_out.reshape(experts, capacity, width),
        "expert",
        split_axis=0,
        concat_axis=0,
        tiled=True,
    ).reshape(slot_total, width)
    first_out = dot_first(pick_first, returned)
    second_out = dot_first(pick_second, returned)
    out = (combine[:, 0:1] * first_out + combine[:, 1:2] * second_out).astype(jnp.bfloat16)
    cot = cotangent.astype(jnp.float32)
    d_combine = jnp.stack(
        [jnp.sum(cot * first_out, axis=1), jnp.sum(cot * second_out, axis=1)], axis=1
    )
    first_cot = (combine[:, 0:1] * cot).astype(jnp.bfloat16)
    second_cot = (combine[:, 1:2] * cot).astype(jnp.bfloat16)
    send_cot = (dot_plain(pick_first, first_cot) + dot_plain(pick_second, second_cot)).astype(
        jnp.bfloat16
    )
    cot_rows = lax.all_to_all(
        send_cot.reshape(experts, capacity, width),
        "expert",
        split_axis=0,
        concat_axis=0,
        tiled=True,
    ).reshape(slot_total, width)
    group_cot = lax.all_gather(cot_rows, "dp", axis=0, tiled=True)
    d_hidden = dot_last(group_cot, local_down)
    d_gate, d_up = gate_grads(d_hidden, gate_pre, up_pre, sigmoid_gate)
    back_terms = dot_last(d_gate, local_gate) + dot_last(d_up, local_up)
    back_rows = lax.psum_scatter(
        back_terms.astype(jnp.bfloat16), "dp", scatter_dimension=0, tiled=True
    )
    grad_gate = group_total(group_rows, d_gate, groups)
    grad_up = group_total(group_rows, d_up, groups)
    grad_down = group_total(hidden, group_cot, groups)
    arrived = lax.all_to_all(
        back_rows.reshape(experts, capacity, width),
        "expert",
        split_axis=0,
        concat_axis=0,
        tiled=True,
    ).reshape(slot_total, width)
    d_tokens = dot_first(pick_both, arrived).astype(jnp.bfloat16)
    return (out, d_tokens, d_combine, grad_gate[None], grad_up[None], grad_down[None])


def on_device(tokens, routes, combine, w_gate, w_up, w_down, cotangent):
    experts = lax.axis_size("expert")
    groups = lax.axis_size("dp")
    count, width = tokens.shape
    capacity = 10 * count // (4 * experts)
    if capacity % 8 or count % 128 or width % 128 or width < 384 or groups % 2:
        return plain_device(tokens, routes, combine, w_gate, w_up, w_down, cotangent)
    meta = jnp.concatenate(
        [routes.astype(jnp.float32).T, combine.T, jnp.zeros((4, count), jnp.float32)], axis=0
    )
    table = (groups, experts, capacity, width)
    tok_all, cot_all, cot_group, meta_all = dispatch(
        groups, experts, capacity, tokens, cotangent, meta
    )
    group_rows = tok_all.reshape(-1, width)
    group_cot = cot_all.reshape(-1, width)
    local_gate = w_gate[0]
    local_up = w_up[0]
    local_down = w_down[0]
    gate_pre = dot_plain(group_rows, local_gate)
    up_pre = dot_plain(group_rows, local_up)
    sigmoid_gate = jax.nn.sigmoid(gate_pre)
    hidden = (gate_pre * sigmoid_gate * up_pre).astype(jnp.bfloat16)
    out_part = dot_plain(hidden, local_down).astype(jnp.bfloat16)
    d_hidden = dot_last(group_cot, local_down)
    d_gate, d_up = gate_grads(d_hidden, gate_pre, up_pre, sigmoid_gate)
    back_part = (dot_last(d_gate, local_gate) + dot_last(d_up, local_up)).astype(jnp.bfloat16)
    out, d_tokens, dots = give_back(
        groups, experts, capacity, out_part.reshape(table), back_part.reshape(table),
        cot_group, meta_all,
    )
    out, d_tokens, d_combine = finish(out, d_tokens, dots)
    grad_gate = dot_first(group_rows, d_gate).astype(jnp.bfloat16)
    grad_up = dot_first(group_rows, d_up).astype(jnp.bfloat16)
    grad_down = dot_first(hidden, group_cot).astype(jnp.bfloat16)
    return (out, d_tokens, d_combine, grad_gate[None], grad_up[None], grad_down[None])


def solution(mesh):
    placed = (
        P(("dp", "expert"), None),
        P(("dp", "expert"), None),
        P(("dp", "expert"), None),
        P("expert", None, "dp"),
        P("expert", None, "dp"),
        P("expert", "dp", None),
        P(("dp", "expert"), None),
    )
    return jax.shard_map(
        on_device,
        mesh=mesh,
        in_specs=placed,
        out_specs=(
            P(("dp", "expert"), None),
            P(("dp", "expert"), None),
            P(("dp", "expert"), None),
            P("expert", None, "dp"),
            P("expert", None, "dp"),
            P("expert", "dp", None),
        ),
        check_vma=False,
    )
```
